128 devices in a mesh: grp: 32 (over y, x, core), mem: 4 (over z).
Axes of the slice: x: 4, y: 4, z: 4, core: 2. Of those that a mesh axis runs over, the one named last changes fastest.
Arguments:
- incident: bfloat16 [2, 256, 65536], P(None, None, ('grp', 'mem')), may hold values from -6 to 6
- near_blocks: bfloat16 [256, 3, 2, 256, 256], P(('grp', 'mem')), may hold values from -0.15625 to 0.15625
- near_mask: int32 [256, 3], P(('grp', 'mem')), may hold values 0 or 1
- far_source: int32 [32, 14], replicated, may hold values from 0 to 31
- far_rank: int32 [32, 14], P('grp'), may hold values from 32 to 128
- basis_in: bfloat16 [32, 4, 14, 2, 128, 512], P('grp', 'mem'), may hold values from -0.1875 to 0.1875
- section_one: bfloat16 [32, 4, 14, 2, 128, 256], P('grp', 'mem'), may hold values from -0.25 to 0.25
- section_two: bfloat16 [32, 4, 14, 2, 128, 256], P('grp', 'mem'), may hold values from -0.25 to 0.25
- basis_out: bfloat16 [32, 4, 14, 2, 2048, 128], P('grp', 'mem'), may hold values from -0.0625 to 0.0625
Outputs:
- product: bfloat16 [2, 256, 65536], P(None, None, ('grp', 'mem'))
The draws below stay inside these ranges and needn't reach their ends.
Inputs may be any that keep to these rules, and one draw needn't show every extreme that they name: far_source names the cluster whose coefficients feed each far-field block; clusters may repeat. far_rank gives the number of live rank components of each block. `near_mask`: 1 marks a present near-field block.
All inputs are finite; a program needn't handle non-finite values.
Results may differ from the reference program's by a relative error of at most 0.0053.
Values may be sent and summed in bfloat16 or wider, within the bound.
No kernel may reach another device: no remote copies, remote signals or barrier semaphores. Data moves between devices by JAX's collectives and lax.ppermute only.
A program may use at most 128 MiB of HBM per device.

```python
import jax
import jax.numpy as jnp
import numpy as np
from jax import lax

ROWS_DEV = 512
NRHS = 256
RANK = 128
LEAF = 256
FAR = 14
GROUPS = 32
MEMBERS = 4
UNKNOWNS = 65536
LEAVES = 256


def plant(result, own_key, smallest, top_value):
    longest = result.shape.index(max(result.shape))
    spots = []
    for shift in (0, 1):
        where = [jax.random.randint(jax.random.fold_in(own_key, axis), (), 0, length) for axis, length in enumerate(result.shape)]
        where[longest] = (where[longest] + shift) % result.shape[longest]
        spots.append(tuple(where))
    return result.at[spots[0]].set(smallest).at[spots[1]].set(top_value)


def level_of(own_key, shape, split, smallest, largest):
    level = 1.0
    for axis_at, shards_of in split:
        heights = jax.random.uniform(jax.random.fold_in(jax.random.fold_in(own_key, 6), axis_at), (shards_of,), jnp.float32, smallest / len(split), largest / len(split))
        level = level * jnp.repeat(jnp.exp(heights), shape[axis_at] // shards_of).reshape((-1,) + (1,) * (len(shape) - 1 - axis_at))
    return level


def centred(stream_key, shape, width, limit, cuts=(), kind=jnp.bfloat16):
    drawn = jax.random.normal(stream_key, shape, jnp.float32) * width
    if len(cuts) > 0:
        drawn = level_of(stream_key, shape, cuts, -0.22, 0.18) * drawn
    return jnp.clip(drawn, min=-limit, max=limit).astype(kind)


def setup_inputs(seed: int = 0) -> dict:
    splits = jax.random.split(jax.random.key(seed), 10)
    return {
        "incident": centred(splits[0], (2, NRHS, UNKNOWNS), 1.0, 6.0, ((2, 128),)),
        "near_blocks": centred(splits[1], (LEAVES, 3, 2, LEAF, LEAF), (6 * LEAF) ** -0.5, 0.15625, ((0, 128),)),
        "near_mask": plant((jax.random.randint(splits[2], (LEAVES, 3), 0, 4) < 3).astype(jnp.int32), jax.random.fold_in(splits[2], 1), 0, 1),
        "far_source": plant(jax.random.randint(splits[3], (GROUPS, FAR), 0, GROUPS), jax.random.fold_in(splits[3], 1), 0, GROUPS - 1).astype(jnp.int32),
        "far_rank": plant(jax.random.randint(splits[4], (GROUPS, FAR), RANK // 4, RANK + 1), jax.random.fold_in(splits[4], 1), RANK // 4, RANK).astype(jnp.int32),
        "basis_in": centred(splits[5], (GROUPS, MEMBERS, FAR, 2, RANK, ROWS_DEV), (2 * ROWS_DEV) ** -0.5, 0.1875, ((0, 32), (1, 4))),
        "section_one": centred(splits[6], (GROUPS, MEMBERS, FAR, 2, RANK, 2 * RANK), (4 * RANK) ** -0.5, 0.25, ((0, 32), (1, 4))),
        "section_two": centred(splits[7], (GROUPS, MEMBERS, FAR, 2, RANK, 2 * RANK), (4 * RANK) ** -0.5, 0.25, ((0, 32), (1, 4))),
        "basis_out": centred(splits[8], (GROUPS, MEMBERS, FAR, 2, MEMBERS * ROWS_DEV, RANK), (4 * RANK * FAR) ** -0.5, 0.0625, ((0, 32), (1, 4))),
    }


def complex_apply(weight_real, weight_imag, vector_real, vector_imag, form):
    def mult(left, right):
        return jnp.einsum(form, left.astype(jnp.float32), right.astype(jnp.float32), precision=lax.Precision.HIGHEST)
    first = mult(weight_real, vector_real) - mult(weight_imag, vector_imag)
    second = mult(weight_real, vector_imag) + mult(weight_imag, vector_real)
    return first, second


def reference(incident, near_blocks, near_mask, far_source, far_rank, basis_in, section_one, section_two, basis_out):
    padded = jnp.pad(incident, ((0, 0), (0, 0), (LEAF, LEAF)))
    near_real = jnp.zeros((NRHS, LEAVES, LEAF), jnp.float32)
    near_imag = jnp.zeros((NRHS, LEAVES, LEAF), jnp.float32)
    for offset in range(3):
        window = padded[:, :, offset * LEAF: offset * LEAF + UNKNOWNS].reshape(2, NRHS, LEAVES, LEAF)
        first, second = complex_apply(near_blocks[:, offset, 0], near_blocks[:, offset, 1], window[0], window[1], "lab,nlb->nla")
        weight = near_mask[:, offset].astype(jnp.float32)[None, :, None]
        near_real = near_real + weight * first
        near_imag = near_imag + weight * second
    near = jnp.stack([near_real.reshape(NRHS, UNKNOWNS), near_imag.reshape(NRHS, UNKNOWNS)], 0)

    pieces = jnp.transpose(incident.reshape(2, NRHS, GROUPS, MEMBERS, ROWS_DEV), (2, 3, 0, 1, 4))
    members = np.arange(MEMBERS)

    def one_group(group):
        chosen = jnp.transpose(pieces[far_source[group]], (1, 0, 2, 3, 4))
        keep = (jnp.arange(RANK)[None, :] < far_rank[group][:, None]).astype(jnp.float32)
        keep = keep[None, :, None, :]
        first, second = complex_apply(basis_in[group][:, :, 0], basis_in[group][:, :, 1], chosen[:, :, 0], chosen[:, :, 1], "mfkr,mfnr->mfnk")
        level = jnp.stack([first * keep, second * keep], 2).astype(jnp.bfloat16)
        for bit, weights in ((0, section_one[group]), (1, section_two[group])):
            lower_index = members & ~(1 << bit)
            upper_index = members | (1 << bit)
            joined = jnp.concatenate([level[lower_index], level[upper_index]], -1)
            first, second = complex_apply(weights[:, :, 0], weights[:, :, 1], joined[:, :, 0], joined[:, :, 1], "mfkj,mfnj->mfnk")
            level = jnp.stack([first * keep, second * keep], 2).astype(jnp.bfloat16)
        outward = basis_out[group]
        first, second = complex_apply(outward[:, :, 0], outward[:, :, 1], level[:, :, 0], level[:, :, 1], "mfrk,mfnk->nr")
        return jnp.stack([first, second], 0)

    far = lax.map(one_group, jnp.arange(GROUPS, dtype=jnp.int32))
    far = jnp.transpose(far, (1, 2, 0, 3)).reshape(2, NRHS, UNKNOWNS)
    return (far + near).astype(jnp.bfloat16)
```

```python
import functools

import jax
import jax.numpy as jnp
from jax import lax
from jax.experimental import pallas as pl
from jax.experimental.pallas import tpu as pltpu
from jax.sharding import PartitionSpec as P

F32 = jnp.float32
BF16 = jnp.bfloat16
ORDERS = ((2, 6, 8, 24), (6, 2, 24, 8), (8, 24, 2, 6), (24, 8, 6, 2))


def swap(value, axis, mask):
    return lax.ppermute(value, axis, [(i, i ^ mask) for i in range(lax.axis_size(axis))])


def nt(left, right):
    return lax.dot_general(left, right, (((1,), (1,)), ((), ())), preferred_element_type=F32)


def call(body, name, grid, prefetch, in_specs, out_specs, out_shape, flops, nbytes, scratch=()):
    return pl.pallas_call(
        body,
        name=name,
        grid_spec=pltpu.PrefetchScalarGridSpec(
            num_scalar_prefetch=prefetch,
            grid=grid,
            in_specs=in_specs,
            out_specs=out_specs,
            scratch_shapes=scratch,
        ),
        out_shape=out_shape,
        compiler_params=pltpu.CompilerParams(dimension_semantics=("arbitrary",) * len(grid)),
        cost_estimate=pl.CostEstimate(flops=flops, bytes_accessed=nbytes, transcendentals=0),
    )


def near_body(mask, x, low, high, blocks, out):
    rows = x.shape[1]
    leaf = blocks.shape[-1]
    left = low[...].reshape(2 * rows, leaf)
    mid = [x[:, :, i * leaf : (i + 1) * leaf].reshape(2 * rows, leaf) for i in range(2)]
    right = high[...].reshape(2 * rows, leaf)
    seq = [left, *mid, right]
    for i in range(2):
        real = jnp.zeros((rows, leaf), F32)
        imag = jnp.zeros((rows, leaf), F32)
        for j in range(3):
            p = nt(seq[i + j], blocks[i, j].reshape(2 * leaf, leaf))
            w = mask[i, j].astype(F32)
            real += w * (p[:rows, :leaf] - p[rows:, leaf:])
            imag += w * (p[rows:, :leaf] + p[:rows, leaf:])
        out[0, :, i * leaf : (i + 1) * leaf] = real
        out[1, :, i * leaf : (i + 1) * leaf] = imag


def near_field(mask, x, low, high, blocks):
    _, nrhs, rows = x.shape
    leaf = blocks.shape[-1]
    q = nrhs // 4
    return call(
        near_body,
        "near",
        (4,),
        1,
        [
            pl.BlockSpec((2, q, rows), lambda i, m: (0, i, 0)),
            pl.BlockSpec((2, q, leaf), lambda i, m: (0, i, 0)),
            pl.BlockSpec((2, q, leaf), lambda i, m: (0, i, 0)),
            pl.BlockSpec(blocks.shape, lambda i, m: (0,) * 5),
        ],
        pl.BlockSpec((2, q, rows), lambda i, m: (0, i, 0)),
        jax.ShapeDtypeStruct((2, nrhs, rows), F32),
        8 * nrhs * 6 * leaf * leaf,
        6 << 20,
    )(mask, x, low, high, blocks)


def place(color, mask):
    def p13(v):
        return v ^ (v >> 1)

    def p31(v):
        return jnp.where(v == 0, 0, jnp.where(v == 3, 1, v + 1))

    a, b = (mask >> 1) & 3, (mask >> 3) & 3
    f = (p13, p31)[color % 2]
    first, second = (a, b) if color < 2 else (b, a)
    p = f(first) + 4 * f(second)
    return 2 * (mask & 1) + (p >> 3), p & 7


def level0_body(colors, base, src, gidx, rank, *refs):
    xs, w, out = refs[:8], refs[8], refs[9]
    f = pl.program_id(0) + base
    mask = src[gidx[0], f] ^ gidx[0]
    parts = []
    for k, color in enumerate(colors):
        which, _ = place(color, mask)
        b = xs[4 * k : 4 * k + 4]
        own = jnp.where(which % 2 == 0, b[0][0], b[1][0])
        other = jnp.where(which % 2 == 0, b[2][0], b[3][0])
        parts.append(jnp.where(which < 2, own, other))
    x = jnp.concatenate(parts, axis=1)
    n = x.shape[1]
    k = w.shape[-2]
    p = nt(x.reshape(2 * n, x.shape[2]), w[0, 0, 0].reshape(2 * k, w.shape[-1]))
    live = lax.broadcasted_iota(jnp.int32, (n, k), 1) < rank[0, f]
    zero = jnp.zeros((n, k), F32)
    out[0, 0] = jnp.where(live, p[:n, :k] - p[n:, k:], zero).astype(BF16)
    out[0, 1] = jnp.where(live, p[n:, :k] + p[:n, k:], zero).astype(BF16)


def level0(colors, base, count, src, gidx, rank, bufs, w):
    _, _, q, rows = bufs[0].shape
    k = w.shape[-2]
    n = 2 * q

    def spec(color, b):
        def index(i, s, g, r):
            which, at = place(color, s[g[0], i + base] ^ g[0])
            return (jnp.where(which == b, at, 0), 0, 0, 0)

        return pl.BlockSpec((1, 2, q, rows), index)

    return call(
        functools.partial(level0_body, colors, base),
        "level0",
        (count,),
        3,
        [spec(c, b) for c in colors for b in range(4)]
        + [pl.BlockSpec((1, 1, 1, 2, k, rows), lambda i, *_: (0, 0, i + base, 0, 0, 0))],
        pl.BlockSpec((1, 2, n, k), lambda i, *_: (i, 0, 0, 0)),
        jax.ShapeDtypeStruct((count, 2, n, k), BF16),
        8 * count * n * k * rows,
        6 << 20,
    )(src, gidx, rank, *bufs, w)


def combine(p, n, k, live):
    zero = jnp.zeros((n, k), F32)
    real = jnp.where(live, p[:n, :k] - p[n:, k:], zero).astype(BF16)
    imag = jnp.where(live, p[n:, :k] + p[:n, k:], zero).astype(BF16)
    return real, imag


def section_body(base, bit, rank, own, other, *refs):
    half = len(refs) // 2
    ws, outs = refs[:half], refs[half:]
    f = pl.program_id(0) + base
    _, _, n, k = own.shape
    a = own[0].reshape(2 * n, k)
    b = other[0].reshape(2 * n, k)
    upper = bit[0] == 1
    x = jnp.concatenate([jnp.where(upper, b, a), jnp.where(upper, a, b)], axis=1)
    live = lax.broadcasted_iota(jnp.int32, (n, k), 1) < rank[0, f]
    for w, out in zip(ws, outs):
        p = nt(x, w[0, 0, 0].reshape(2 * k, 2 * k))
        out[0, 0], out[0, 1] = combine(p, n, k, live)


def section(name, base, bit, rank, own, other, ws):
    count, _, n, k = own.shape
    level = pl.BlockSpec((1, 2, n, k), lambda i, *_: (i, 0, 0, 0))
    shape = jax.ShapeDtypeStruct(own.shape, BF16)
    return call(
        functools.partial(section_body, base),
        name,
        (count,),
        2,
        [level, level]
        + [pl.BlockSpec((1, 1, 1, 2, k, 2 * k), lambda i, *_: (0, 0, i + base, 0, 0, 0))] * len(ws),
        [level] * len(ws),
        [shape] * len(ws),
        16 * count * n * k * k * len(ws),
        (3 + len(ws)) << 20,
    )(bit, rank, own, other, *ws)


def outward_body(dtype, order, *refs):
    levels, w, out, xs = refs[:-3], refs[-3], refs[-2], refs[-1]
    _, _, n, k = levels[0].shape

    @pl.when((pl.program_id(0) == 0) & (pl.program_id(1) == 0))
    def _():
        f = 0
        for level in levels:
            for i in range(level.shape[0]):
                real, imag = level[i, 0], level[i, 1]
                xs[f] = jnp.concatenate(
                    [jnp.concatenate([real, -imag], 1), jnp.concatenate([imag, real], 1)], 0
                )
                f += 1

    rows = w.shape[-2]
    acc = jnp.zeros((2 * n, rows), F32)
    for f in range(xs.shape[0]):
        acc += nt(xs[f], jnp.concatenate([w[0, 0, f, 0], w[0, 0, f, 1]], 1))
    out[0] = acc.reshape(2, n, rows).astype(dtype)


def outward(dtype, order, quarter, levels, w, step=256):
    count, _, n, k = levels[0].shape
    q = n // 2
    far = w.shape[2]
    piece = w.shape[4] // 4
    per = piece // step
    return call(
        functools.partial(outward_body, dtype),
        "outward",
        (2, per),
        1,
        [pl.BlockSpec((v.shape[0], 2, q, k), lambda p, i, o: (0, 0, quarter, 0)) for v in levels]
        + [
            pl.BlockSpec(
                (1, 1, far, 2, step, k), lambda p, i, o: (0, 0, 0, 0, o[p] * per + i, 0)
            )
        ],
        pl.BlockSpec((1, 2, q, step), lambda p, i, o: (p, 0, 0, i)),
        jax.ShapeDtypeStruct((2, 2, q, piece), dtype),
        8 * far * q * k * piece * 2,
        8 << 20,
        [pltpu.VMEM((far, 2 * q, 2 * k), BF16)],
    )(order, *levels, w)


def on_device(
    incident,
    near_blocks,
    near_mask,
    far_source,
    far_rank,
    basis_in,
    section_one,
    section_two,
    basis_out,
):
    _, nrhs, rows = incident.shape
    leaf = near_blocks.shape[3]
    far = basis_in.shape[2]
    q = nrhs // 4
    group = lax.axis_index("grp")
    member = lax.axis_index("mem")
    gidx = group.reshape(1).astype(jnp.int32)

    held = [incident[None, :, c * q : (c + 1) * q] for c in range(4)]
    got = [None] * 4
    for step in range(4):
        got = [swap(held[c], "grp", ORDERS[c][step]) for c in range(4)]
        if step < 3:
            held = [jnp.concatenate([held[c], got[c]], 0) for c in range(4)]
    bufs = [(held[c], got[c], swap(held[c], "grp", 1), swap(got[c], "grp", 1)) for c in range(4)]

    section_pair = swap(section_one, "mem", 1)

    axes = ("grp", "mem")
    total = lax.axis_size("grp") * lax.axis_size("mem")
    forward = [(i, i + 1) for i in range(total - 1)]
    backward = [(i + 1, i) for i in range(total - 1)]
    low = lax.ppermute(incident[:, :, rows - leaf :], axes, forward)
    high = lax.ppermute(incident[:, :, :leaf], axes, backward)
    near = near_field(near_mask, incident, low, high, near_blocks)

    bit0 = (member % 2).reshape(1).astype(jnp.int32)
    bit1 = (member // 2).reshape(1).astype(jnp.int32)
    send_order = jnp.stack([member ^ 3, member ^ 2]).astype(jnp.int32)
    keep_order = jnp.stack([member, member ^ 1]).astype(jnp.int32)
    cut = far // 2
    spans = ((0, cut), (cut, far - cut))

    pieces = []
    for h in range(2):
        colors = (2 * h, 2 * h + 1)
        two = []
        for base, count in spans:
            lev0 = level0(
                colors, base, count, far_source, gidx, far_rank,
                bufs[colors[0]] + bufs[colors[1]], basis_in,
            )
            lev0_pair = swap(lev0, "mem", 1)
            lev1, lev1_pair = section(
                "level1", base, bit0, far_rank, lev0, lev0_pair, [section_one, section_pair]
            )
            lev1_other = swap(lev1_pair, "mem", 3)
            two += section("level2", base, bit1, far_rank, lev1, lev1_other, [section_two])
        for quarter in range(2):
            sent = swap(outward(BF16, send_order, quarter, two, basis_out), "mem", 3)
            kept = outward(F32, keep_order, quarter, two, basis_out)
            last = swap((kept[1] + sent[1].astype(F32)).astype(BF16), "mem", 1)
            at = (2 * h + quarter) * q
            pieces.append(
                (kept[0] + sent[0].astype(F32) + last.astype(F32) + near[:, at : at + q]).astype(BF16)
            )
    return jnp.concatenate(pieces, 1)


def solution(mesh):
    placed = (
        P(None, None, ("grp", "mem")),
        P(("grp", "mem"), None, None, None, None),
        P(("grp", "mem"), None),
        P(),
        P("grp", None),
        P("grp", "mem", None, None, None, None),
        P("grp", "mem", None, None, None, None),
        P("grp", "mem", None, None, None, None),
        P("grp", "mem", None, None, None, None),
    )
    return jax.shard_map(
        on_device,
        mesh=mesh,
        in_specs=placed,
        out_specs=P(None, None, ("grp", "mem")),
        check_vma=False,
    )
```

```python
import functools

import jax
import jax.numpy as jnp
from jax import lax
from jax.experimental import pallas as pl
from jax.experimental.pallas import tpu as pltpu
from jax.sharding import PartitionSpec as P


F32 = jnp.float32
BF16 = jnp.bfloat16
SIDE = 4
SHIFT = {"x": 1, "y": 3}


def swap(value, axis, mask):
    return lax.ppermute(value, axis, [(i, i ^ mask) for i in range(lax.axis_size(axis))])


def ring(value, axis, by):
    at = SHIFT[axis]
    perm = []
    for i in range(lax.axis_size("grp")):
        v = (i >> at) & (SIDE - 1)
        perm.append((i, i + ((((v + by) % SIDE) - v) << at)))
    return lax.ppermute(value, "grp", perm)


def nt(left, right):
    return lax.dot_general(left, right, (((1,), (1,)), ((), ())), preferred_element_type=F32)


VMEM = pl.BlockSpec(memory_space=pltpu.VMEM)
SMEM = pl.BlockSpec(memory_space=pltpu.SMEM)


def size(v):
    return v.size * v.dtype.itemsize


def call(body, scalars, arrays, out_shape, flops, nbytes, scratch=()):
    room = sum(size(v) for v in (*arrays, *jax.tree.leaves(out_shape))) + (2 << 20)
    return pl.pallas_call(
        body,
        in_specs=[SMEM] * len(scalars) + [VMEM] * len(arrays),
        out_specs=jax.tree.map(lambda _: VMEM, out_shape),
        out_shape=out_shape,
        scratch_shapes=scratch,
        compiler_params=pltpu.CompilerParams(vmem_limit_bytes=room),
        cost_estimate=pl.CostEstimate(flops=flops, bytes_accessed=nbytes, transcendentals=0),
    )(*scalars, *arrays)


def near_body(mask, x, low, high, blocks, out):
    nrhs = x.shape[1]
    leaf = blocks.shape[-1]
    rows = nrhs // 4

    def step(t, carry):
        at = pl.ds(pl.multiple_of(t * rows, rows), rows)
        seq = [low[:, at, :]]
        seq += [x[:, at, i * leaf : (i + 1) * leaf] for i in range(2)]
        seq += [high[:, at, :]]
        seq = [v.reshape(2 * rows, leaf) for v in seq]
        for i in range(2):
            real = jnp.zeros((rows, leaf), F32)
            imag = jnp.zeros((rows, leaf), F32)
            for j in range(3):
                p = nt(seq[i + j], blocks[i, j].reshape(2 * leaf, leaf))
                w = mask[i, j].astype(F32)
                real += w * (p[:rows, :leaf] - p[rows:, leaf:])
                imag += w * (p[rows:, :leaf] + p[:rows, leaf:])
            out[0, at, i * leaf : (i + 1) * leaf] = real
            out[1, at, i * leaf : (i + 1) * leaf] = imag
        return carry

    lax.fori_loop(0, 4, step, 0)


def near_field(mask, x, low, high, blocks):
    _, nrhs, rows = x.shape
    leaf = blocks.shape[-1]
    return call(
        near_body, [mask], [x, low, high, blocks],
        jax.ShapeDtypeStruct((2, nrhs, rows), F32),
        8 * nrhs * 6 * leaf * leaf, 4 << 20,
    )


def level0_body(color, base, count, src, gidx, rank, *refs):
    bufs, w, out, xs = refs[:10], refs[10], refs[11], refs[12]
    me = gidx[0]
    k = w.shape[-2]
    n = xs.shape[1]

    def step(i, carry):
        f = i + base
        s = src[me, f]
        dx = (((s >> 1) & 3) - ((me >> 1) & 3)) & 3
        dy = (((s >> 3) & 3) - ((me >> 3) & 3)) & 3
        first, second = (dx, dy) if color == 0 else (dy, dx)
        p = jnp.where(first == 0, 0, jnp.where(first == 3, 1, first + 1))
        b = jnp.where(second == 0, 0, jnp.where(second == 3, 1, jnp.where(second == 1, 2, 3 + (p >> 1))))
        at = jnp.where(b >= 3, p & 1, p)
        which = b + 5 * ((s ^ me) & 1)
        for t in range(10):

            @pl.when(which == t)
            def _():
                xs[...] = bufs[t][at]

        x = xs[...].reshape(2 * n, xs.shape[2])
        p = nt(x, w[0, 0, f].reshape(2 * k, w.shape[-1]))
        live = lax.broadcasted_iota(jnp.int32, (n, k), 1) < rank[0, f]
        real, imag = combine(p, n, k, live)
        out[i, 0] = real
        out[i, 1] = imag
        return carry

    lax.fori_loop(0, count, step, 0)


def level0(color, base, count, src, gidx, rank, bufs, w):
    _, _, n, rows = bufs[0].shape
    k = w.shape[-2]
    return call(
        functools.partial(level0_body, color, base, count),
        [src, gidx, rank], [*bufs, w],
        jax.ShapeDtypeStruct((count, 2, n, k), BF16),
        8 * count * n * k * rows, 2 << 20,
        [pltpu.VMEM((2, n, rows), BF16)],
    )


def combine(p, n, k, live):
    zero = jnp.zeros((n, k), F32)
    real = jnp.where(live, p[:n, :k] - p[n:, k:], zero).astype(BF16)
    imag = jnp.where(live, p[n:, :k] + p[:n, k:], zero).astype(BF16)
    return real, imag


def section_body(base, bit, rank, own, other, *refs):
    half = len(refs) // 2
    ws, outs = refs[:half], refs[half:]
    count, _, n, k = own.shape
    upper = bit[0] == 1
    for i in range(count):
        a = own[i].reshape(2 * n, k)
        b = other[i].reshape(2 * n, k)
        x = jnp.concatenate([jnp.where(upper, b, a), jnp.where(upper, a, b)], axis=1)
        live = lax.broadcasted_iota(jnp.int32, (n, k), 1) < rank[0, base + i]
        for w, out in zip(ws, outs):
            p = nt(x, w[0, 0, base + i].reshape(2 * k, 2 * k))
            out[i, 0], out[i, 1] = combine(p, n, k, live)


def section(base, bit, rank, own, other, ws):
    count, _, n, k = own.shape
    shape = jax.ShapeDtypeStruct(own.shape, BF16)
    return call(
        functools.partial(section_body, base),
        [bit, rank], [own, other, *ws], [shape] * len(ws),
        16 * count * n * k * k * len(ws), 2 << 20,
    )


def outward_body(dtype, quarter, order, *refs):
    levels, w, out, xs = refs[:-3], refs[-3], refs[-2], refs[-1]
    n = xs.shape[1] // 2
    rhs = slice(quarter * n, quarter * n + n)
    f = 0
    for level in levels:
        for i in range(level.shape[0]):
            real, imag = level[i, 0, rhs], level[i, 1, rhs]
            xs[f, :n] = jnp.concatenate([real, -imag], 1)
            xs[f, n:] = jnp.concatenate([imag, real], 1)
            f += 1
    step = 256
    piece = w.shape[4] // 4
    for p in range(2):

        def body(i, carry):
            start = pl.multiple_of(order[p] * piece + i * step, step)
            rows = pl.ds(start, step)
            acc = jnp.zeros((2 * n, step), F32)
            for f in range(xs.shape[0]):
                acc += nt(xs[f], jnp.concatenate([w[0, 0, f, 0, rows], w[0, 0, f, 1, rows]], 1))
            to = pl.ds(pl.multiple_of(i * step, step), step)
            out[p, 0, :, to] = acc[:n].astype(dtype)
            out[p, 1, :, to] = acc[n:].astype(dtype)
            return carry

        lax.fori_loop(0, piece // step, body, 0)


def outward(dtype, order, quarter, levels, w):
    _, _, n, k = levels[0].shape
    q = n // 2
    far = w.shape[2]
    piece = w.shape[4] // 4
    return call(
        functools.partial(outward_body, dtype, quarter),
        [order], [*levels, w],
        jax.ShapeDtypeStruct((2, 2, q, piece), dtype),
        8 * far * q * k * piece * 2, 4 << 20,
        [pltpu.VMEM((far, 2 * q, 2 * k), BF16)],
    )


def gather(color, block):
    one, two = ("x", "y") if color == 0 else ("y", "x")
    below = ring(block, one, 1)
    above = ring(block, one, -1)
    far_r = ring(below[:, :1], one, 1)
    far_i = ring(above[:, 1:], one, -1)
    line = jnp.concatenate([block, below, above, jnp.concatenate([far_r, far_i], 1)], 0)
    below = ring(line, two, 1)
    above = ring(line, two, -1)
    far_lo = ring(below[:2], two, 1)
    far_hi = ring(above[2:], two, -1)
    mine = [line, below, above, far_lo, far_hi]
    return mine + [swap(v, "grp", 1) for v in mine]


def on_device(
    incident,
    near_blocks,
    near_mask,
    far_source,
    far_rank,
    basis_in,
    section_one,
    section_two,
    basis_out,
):
    _, nrhs, rows = incident.shape
    leaf = near_blocks.shape[3]
    far = basis_in.shape[2]
    q = nrhs // 4
    member = lax.axis_index("mem")
    gidx = lax.axis_index("grp").reshape(1).astype(jnp.int32)

    bufs = [gather(c, incident[None, :, 2 * c * q : 2 * (c + 1) * q]) for c in range(2)]
    section_pair = swap(section_one, "mem", 1)

    axes = ("grp", "mem")
    total = lax.axis_size("grp") * lax.axis_size("mem")
    forward = [(i, i + 1) for i in range(total - 1)]
    backward = [(i + 1, i) for i in range(total - 1)]
    low = lax.ppermute(incident[:, :, rows - leaf :], axes, forward)
    high = lax.ppermute(incident[:, :, :leaf], axes, backward)
    near = near_field(near_mask, incident, low, high, near_blocks)

    bit0 = (member & 1).reshape(1).astype(jnp.int32)
    bit1 = (member >> 1).reshape(1).astype(jnp.int32)
    send_order = (member ^ jnp.array([1, 2])).astype(jnp.int32)
    keep_order = (member ^ jnp.array([0, 3])).astype(jnp.int32)
    cut = far // 2
    spans = ((0, cut), (cut, far - cut))

    pieces = []
    for h in range(2):
        two = []
        for base, count in spans:
            lev0 = level0(h, base, count, far_source, gidx, far_rank, bufs[h], basis_in)
            lev0_pair = swap(lev0, "mem", 1)
            lev1, lev1_pair = section(
                base, bit0, far_rank, lev0, lev0_pair, [section_one, section_pair]
            )
            lev1_other = swap(lev1_pair, "mem", 3)
            two += section(base, bit1, far_rank, lev1, lev1_other, [section_two])
        for quarter in range(2):
            sent = outward(BF16, send_order, quarter, two, basis_out)
            sent = swap(sent, "mem", 1)
            kept = outward(F32, keep_order, quarter, two, basis_out)
            last = (kept[1] + sent[1].astype(F32)).astype(BF16)
            last = swap(last, "mem", 3)
            at = (2 * h + quarter) * q
            pieces.append(
                (kept[0] + sent[0].astype(F32) + last.astype(F32) + near[:, at : at + q]).astype(BF16)
            )
    return jnp.concatenate(pieces, 1)


def solution(mesh):
    placed = (
        P(None, None, ("grp", "mem")),
        P(("grp", "mem"), None, None, None, None),
        P(("grp", "mem"), None),
        P(),
        P("grp", None),
        P("grp", "mem", None, None, None, None),
        P("grp", "mem", None, None, None, None),
        P("grp", "mem", None, None, None, None),
        P("grp", "mem", None, None, None, None),
    )

    return jax.shard_map(
        on_device,
        mesh=mesh,
        in_specs=placed,
        out_specs=P(None, None, ("grp", "mem")),
        check_vma=False,
    )
```

```python
import functools

import jax
import jax.numpy as jnp
from jax import lax
from jax.experimental import pallas as pl
from jax.experimental.pallas import tpu as pltpu
from jax.sharding import PartitionSpec as P


F32 = jnp.float32
BF16 = jnp.bfloat16
SIDE = 4
SHIFT = {"x": 1, "y": 3}


def swap(value, axis, mask):
    return lax.ppermute(value, axis, [(i, i ^ mask) for i in range(lax.axis_size(axis))])


def ring(value, axis, by):
    at = SHIFT[axis]
    perm = []
    for i in range(lax.axis_size("grp")):
        v = (i >> at) & (SIDE - 1)
        perm.append((i, i + ((((v + by) % SIDE) - v) << at)))
    return lax.ppermute(value, "grp", perm)


def nt(left, right):
    return lax.dot_general(left, right, (((1,), (1,)), ((), ())), preferred_element_type=F32)


VMEM = pl.BlockSpec(memory_space=pltpu.VMEM)
SMEM = pl.BlockSpec(memory_space=pltpu.SMEM)


def size(v):
    return v.size * v.dtype.itemsize


def call(body, scalars, arrays, out_shape, flops, nbytes, scratch=(), space=None, room=0):
    space = space or [pltpu.VMEM] * len(arrays)
    inside = [v for v, at in zip(arrays, space) if at == pltpu.VMEM]
    room += sum(size(v) for v in jax.tree.leaves(out_shape) + inside) + (2 << 20)
    return pl.pallas_call(
        body,
        in_specs=[SMEM] * len(scalars) + [pl.BlockSpec(memory_space=at) for at in space],
        out_specs=jax.tree.map(lambda _: VMEM, out_shape),
        out_shape=out_shape,
        scratch_shapes=scratch,
        compiler_params=pltpu.CompilerParams(vmem_limit_bytes=room),
        cost_estimate=pl.CostEstimate(flops=flops, bytes_accessed=nbytes, transcendentals=0),
    )(
        *scalars,
        *(
            pltpu.with_memory_space_constraint(v, at) if at == pltpu.HBM else v
            for v, at in zip(arrays, space)
        ),
    )


def near_body(mask, x, low, high, blocks, out):
    nrhs = x.shape[1]
    leaf = blocks.shape[-1]
    rows = nrhs // 4

    def step(t, carry):
        at = pl.ds(pl.multiple_of(t * rows, rows), rows)
        seq = [low[:, at, :]]
        seq += [x[:, at, i * leaf : (i + 1) * leaf] for i in range(2)]
        seq += [high[:, at, :]]
        seq = [v.reshape(2 * rows, leaf) for v in seq]
        for i in range(2):
            real = jnp.zeros((rows, leaf), F32)
            imag = jnp.zeros((rows, leaf), F32)
            for j in range(3):
                p = nt(seq[i + j], blocks[i, j].reshape(2 * leaf, leaf))
                w = mask[i, j].astype(F32)
                real += w * (p[:rows, :leaf] - p[rows:, leaf:])
                imag += w * (p[rows:, :leaf] + p[:rows, leaf:])
            out[0, at, i * leaf : (i + 1) * leaf] = real
            out[1, at, i * leaf : (i + 1) * leaf] = imag
        return carry

    lax.fori_loop(0, 4, step, 0)


def near_field(mask, x, low, high, blocks):
    _, nrhs, rows = x.shape
    leaf = blocks.shape[-1]
    return call(
        near_body, [mask], [x, low, high, blocks],
        jax.ShapeDtypeStruct((2, nrhs, rows), F32),
        8 * nrhs * 6 * leaf * leaf, 4 << 20,
    )


def level0_body(color, base, count, src, gidx, rank, *refs):
    bufs, w, out = refs[:16], refs[16], refs[17]
    xs, ws, sems = refs[18:]
    me = gidx[0]
    k = w.shape[-2]
    n = xs.shape[2]

    def fetch(i, carry):
        f = i + base
        s = src[me, f]
        dx = (((s >> 1) & 3) - ((me >> 1) & 3)) & 3
        dy = (((s >> 3) & 3) - ((me >> 3) & 3)) & 3
        dx, dy = (jnp.where(v == 0, 0, jnp.where(v == 3, 1, v + 1)) for v in (dx, dy))
        first, second = (dx, dy) if color == 0 else (dy, dx)
        which = 2 * second + (first >> 1) + 8 * ((s ^ me) & 1)
        for t in range(16):

            @pl.when(which == t)
            def _():
                pltpu.make_async_copy(bufs[t].at[first & 1], xs.at[i], sems.at[0, i]).start()

        pltpu.make_async_copy(w.at[0, 0, f], ws.at[i], sems.at[1, i]).start()
        return carry

    lax.fori_loop(0, count, fetch, 0)
    for i in range(count):
        pltpu.make_async_copy(bufs[0].at[0], xs.at[i], sems.at[0, i]).wait()
        pltpu.make_async_copy(w.at[0, 0, 0], ws.at[i], sems.at[1, i]).wait()
        p = nt(xs[i].reshape(2 * n, xs.shape[3]), ws[i].reshape(2 * k, ws.shape[3]))
        live = lax.broadcasted_iota(jnp.int32, (n, k), 1) < rank[0, base + i]
        out[i, 0], out[i, 1] = combine(p, n, k, live)


def level0(color, base, count, src, gidx, rank, bufs, w):
    _, _, n, rows = bufs[0].shape
    k = w.shape[-2]
    return call(
        functools.partial(level0_body, color, base, count),
        [src, gidx, rank], [*bufs, w],
        jax.ShapeDtypeStruct((count, 2, n, k), BF16),
        8 * count * n * k * rows, 4 << 20,
        [
            pltpu.VMEM((count, 2, n, rows), BF16),
            pltpu.VMEM((count, 2, k, rows), BF16),
            pltpu.SemaphoreType.DMA((2, count)),
        ],
        space=[pltpu.HBM] * 17,
        room=count * 2 * rows * (n + k) * 2,
    )


def combine(p, n, k, live):
    zero = jnp.zeros((n, k), F32)
    real = jnp.where(live, p[:n, :k] - p[n:, k:], zero).astype(BF16)
    imag = jnp.where(live, p[n:, :k] + p[:n, k:], zero).astype(BF16)
    return real, imag


def section_body(base, bit, rank, own, other, *refs):
    half = len(refs) // 2
    ws, outs = refs[:half], refs[half:]
    count, _, n, k = own.shape
    upper = bit[0] == 1
    for i in range(count):
        a = own[i].reshape(2 * n, k)
        b = other[i].reshape(2 * n, k)
        x = jnp.concatenate([jnp.where(upper, b, a), jnp.where(upper, a, b)], axis=1)
        live = lax.broadcasted_iota(jnp.int32, (n, k), 1) < rank[0, base + i]
        for w, out in zip(ws, outs):
            p = nt(x, w[0, 0, base + i].reshape(2 * k, 2 * k))
            out[i, 0], out[i, 1] = combine(p, n, k, live)


def section(base, bit, rank, own, other, ws):
    count, _, n, k = own.shape
    shape = jax.ShapeDtypeStruct(own.shape, BF16)
    return call(
        functools.partial(section_body, base),
        [bit, rank], [own, other, *ws], [shape] * len(ws),
        16 * count * n * k * k * len(ws), 2 << 20,
    )


def outward_body(dtype, order, *refs):
    levels, w, out, xs, ws, sems = refs[:-5], refs[-5], refs[-4], refs[-3], refs[-2], refs[-1]
    n = xs.shape[1] // 2
    blocks, step = ws.shape[0], ws.shape[3]
    piece = out.shape[3]
    per = piece // step

    def copy(b):
        start = pl.multiple_of(order[b // per] * piece + (b % per) * step, step)
        return pltpu.make_async_copy(w.at[0, 0, :, :, pl.ds(start, step)], ws.at[b], sems.at[b])

    copy(0).start()
    copy(1).start()
    f = 0
    for level in levels:
        for i in range(level.shape[0]):
            real, imag = level[i, 0], level[i, 1]
            xs[f, :n] = jnp.concatenate([real, -imag], 1)
            xs[f, n:] = jnp.concatenate([imag, real], 1)
            f += 1

    def body(b, carry):
        copy(b).wait()

        @pl.when(b + 2 < blocks)
        def _():
            copy(b + 2).start()

        acc = jnp.zeros((2 * n, step), F32)
        for f in range(xs.shape[0]):
            acc += nt(xs[f], jnp.concatenate([ws[b, f, 0], ws[b, f, 1]], 1))
        to = pl.ds(pl.multiple_of((b % per) * step, step), step)
        out[b // per, 0, :, to] = acc[:n].astype(dtype)
        out[b // per, 1, :, to] = acc[n:].astype(dtype)
        return carry

    lax.fori_loop(0, blocks, body, 0)


def outward(dtype, order, levels, w, step=256):
    _, _, n, k = levels[0].shape
    far = w.shape[2]
    piece = w.shape[4] // 4
    count = order.shape[0]
    blocks = count * piece // step
    return call(
        functools.partial(outward_body, dtype),
        [order], [*levels, w],
        jax.ShapeDtypeStruct((count, 2, n, piece), dtype),
        8 * far * n * k * piece * count, 4 << 20,
        [
            pltpu.VMEM((far, 2 * n, 2 * k), BF16),
            pltpu.VMEM((blocks, far, 2, step, k), BF16),
            pltpu.SemaphoreType.DMA((blocks,)),
        ],
        space=[pltpu.VMEM] * len(levels) + [pltpu.HBM],
        room=far * n * k * 8 + blocks * far * step * k * 4,
    )


def gather(color, block):
    one, two = ("x", "y") if color == 0 else ("y", "x")
    below = ring(block, one, 1)
    above = ring(block, one, -1)
    far_r = ring(below[:, :1], one, 1)
    far_i = ring(above[:, 1:], one, -1)
    lo = jnp.concatenate([block, below], 0)
    hi = jnp.concatenate([above, jnp.concatenate([far_r, far_i], 1)], 0)
    below_lo = ring(lo, two, 1)
    above_hi = ring(hi, two, -1)
    below_hi = ring(hi, two, 1)
    above_lo = ring(lo, two, -1)
    far_lo = ring(below_lo, two, 1)
    far_hi = ring(above_hi, two, -1)
    mine = [lo, hi, below_lo, below_hi, above_lo, above_hi, far_lo, far_hi]
    return mine + [swap(v, "grp", 1) for v in mine]


def on_device(
    incident,
    near_blocks,
    near_mask,
    far_source,
    far_rank,
    basis_in,
    section_one,
    section_two,
    basis_out,
):
    _, nrhs, rows = incident.shape
    leaf = near_blocks.shape[3]
    far = basis_in.shape[2]
    q = nrhs // 4
    member = lax.axis_index("mem")
    gidx = lax.axis_index("grp").reshape(1).astype(jnp.int32)

    bufs = [gather(c, incident[None, :, 2 * c * q : 2 * (c + 1) * q]) for c in range(2)]
    section_pair = swap(section_one, "mem", 1)

    axes = ("grp", "mem")
    total = lax.axis_size("grp") * lax.axis_size("mem")
    forward = [(i, i + 1) for i in range(total - 1)]
    backward = [(i + 1, i) for i in range(total - 1)]
    low = lax.ppermute(incident[:, :, rows - leaf :], axes, forward)
    high = lax.ppermute(incident[:, :, :leaf], axes, backward)
    near = near_field(near_mask, incident, low, high, near_blocks)

    bit0 = (member & 1).reshape(1).astype(jnp.int32)
    bit1 = (member >> 1).reshape(1).astype(jnp.int32)
    far_near = jnp.array([2, 1, 3, 0], jnp.int32)
    cut = far // 2
    spans = ((0, cut), (cut, far - cut))

    pieces = []
    for h in range(2):
        two = []
        for base, count in spans:
            lev0 = level0(h, base, count, far_source, gidx, far_rank, bufs[h], basis_in)
            lev0_pair = swap(lev0, "mem", 1)
            lev1, lev1_pair = section(
                base, bit0, far_rank, lev0, lev0_pair, [section_one, section_pair]
            )
            lev1_other = swap(lev1_pair, "mem", 3)
            two += section(base, bit1, far_rank, lev1, lev1_other, [section_two])
        if h == 0:
            sent = outward(BF16, member ^ far_near[:2], two, basis_out)
            sent = swap(sent, "mem", 1)
            sent = (sent[0], sent[1])
        else:
            sent = []
            for i in range(2):
                part = outward(BF16, member ^ far_near[i : i + 1], two, basis_out)
                sent.append(swap(part, "mem", 1)[0])
        other = outward(F32, member ^ far_near[2:3], two, basis_out)[0]
        last = swap((other + sent[0].astype(F32)).astype(BF16), "mem", 3)
        kept = outward(F32, member ^ far_near[3:], two, basis_out)[0]
        at = slice(2 * h * q, 2 * (h + 1) * q)
        pieces.append((kept + sent[1].astype(F32) + last.astype(F32) + near[:, at]).astype(BF16))
    return jnp.concatenate(pieces, 1)


def solution(mesh):
    placed = (
        P(None, None, ("grp", "mem")),
        P(("grp", "mem"), None, None, None, None),
        P(("grp", "mem"), None),
        P(),
        P("grp", None),
        P("grp", "mem", None, None, None, None),
        P("grp", "mem", None, None, None, None),
        P("grp", "mem", None, None, None, None),
        P("grp", "mem", None, None, None, None),
    )

    return jax.shard_map(
        on_device,
        mesh=mesh,
        in_specs=placed,
        out_specs=P(None, None, ("grp", "mem")),
        check_vma=False,
    )
```

```python
import functools

import jax
import jax.numpy as jnp
from jax import lax
from jax.experimental import pallas as pl
from jax.experimental.pallas import tpu as pltpu
from jax.sharding import PartitionSpec as P


F32 = jnp.float32
BF16 = jnp.bfloat16
SIDE = 4
SHIFT = {"x": 1, "y": 3}


def swap(value, axis, mask):
    return lax.ppermute(value, axis, [(i, i ^ mask) for i in range(lax.axis_size(axis))])


def ring(value, axis, by):
    at = SHIFT[axis]
    perm = []
    for i in range(lax.axis_size("grp")):
        v = (i >> at) & (SIDE - 1)
        perm.append((i, i + ((((v + by) % SIDE) - v) << at)))
    return lax.ppermute(value, "grp", perm)


def nt(left, right):
    return lax.dot_general(left, right, (((1,), (1,)), ((), ())), preferred_element_type=F32)


VMEM = pl.BlockSpec(memory_space=pltpu.VMEM)
SMEM = pl.BlockSpec(memory_space=pltpu.SMEM)


def size(v):
    return v.size * v.dtype.itemsize


def call(body, scalars, arrays, out_shape, flops, nbytes, scratch=(), space=None, room=0):
    space = space or [pltpu.VMEM] * len(arrays)
    inside = [v for v, at in zip(arrays, space) if at == pltpu.VMEM]
    room += sum(size(v) for v in jax.tree.leaves(out_shape) + inside) + (2 << 20)
    return pl.pallas_call(
        body,
        in_specs=[SMEM] * len(scalars) + [pl.BlockSpec(memory_space=at) for at in space],
        out_specs=jax.tree.map(lambda _: VMEM, out_shape),
        out_shape=out_shape,
        scratch_shapes=scratch,
        compiler_params=pltpu.CompilerParams(vmem_limit_bytes=room),
        cost_estimate=pl.CostEstimate(flops=flops, bytes_accessed=nbytes, transcendentals=0),
    )(
        *scalars,
        *(
            pltpu.with_memory_space_constraint(v, at) if at == pltpu.HBM else v
            for v, at in zip(arrays, space)
        ),
    )


def near_body(mask, x, low, high, blocks, out):
    nrhs = x.shape[1]
    leaf = blocks.shape[-1]
    rows = nrhs // 4

    def step(t, carry):
        at = pl.ds(pl.multiple_of(t * rows, rows), rows)
        seq = [low[:, at, :]]
        seq += [x[:, at, i * leaf : (i + 1) * leaf] for i in range(2)]
        seq += [high[:, at, :]]
        seq = [v.reshape(2 * rows, leaf) for v in seq]
        for i in range(2):
            real = jnp.zeros((rows, leaf), F32)
            imag = jnp.zeros((rows, leaf), F32)
            for j in range(3):
                p = nt(seq[i + j], blocks[i, j].reshape(2 * leaf, leaf))
                w = mask[i, j].astype(F32)
                real += w * (p[:rows, :leaf] - p[rows:, leaf:])
                imag += w * (p[rows:, :leaf] + p[:rows, leaf:])
            out[0, at, i * leaf : (i + 1) * leaf] = real
            out[1, at, i * leaf : (i + 1) * leaf] = imag
        return carry

    lax.fori_loop(0, 4, step, 0)


def near_field(mask, x, low, high, blocks):
    _, nrhs, rows = x.shape
    leaf = blocks.shape[-1]
    return call(
        near_body, [mask], [x, low, high, blocks],
        jax.ShapeDtypeStruct((2, nrhs, rows), F32),
        8 * nrhs * 6 * leaf * leaf, 4 << 20,
    )


def level0_body(color, base, count, src, gidx, rank, *refs):
    bufs, w, out = refs[:16], refs[16], refs[17]
    xs, ws, sems = refs[18:]
    me = gidx[0]
    k = w.shape[-2]
    n = xs.shape[2]

    def fetch(i, carry):
        f = i + base
        s = src[me, f]
        dx = (((s >> 1) & 3) - ((me >> 1) & 3)) & 3
        dy = (((s >> 3) & 3) - ((me >> 3) & 3)) & 3
        dx, dy = (jnp.where(v == 0, 0, jnp.where(v == 3, 1, v + 1)) for v in (dx, dy))
        first, second = (dx, dy) if color == 0 else (dy, dx)
        which = 2 * second + (first >> 1) + 8 * ((s ^ me) & 1)
        for t in range(16):

            @pl.when(which == t)
            def _():
                pltpu.make_async_copy(bufs[t].at[first & 1], xs.at[i], sems.at[0, i]).start()

        pltpu.make_async_copy(w.at[0, 0, f], ws.at[i], sems.at[1, i]).start()
        return carry

    lax.fori_loop(0, count, fetch, 0)
    for i in range(count):
        pltpu.make_async_copy(bufs[0].at[0], xs.at[i], sems.at[0, i]).wait()
        pltpu.make_async_copy(w.at[0, 0, 0], ws.at[i], sems.at[1, i]).wait()
        p = nt(xs[i].reshape(2 * n, xs.shape[3]), ws[i].reshape(2 * k, ws.shape[3]))
        live = lax.broadcasted_iota(jnp.int32, (n, k), 1) < rank[0, base + i]
        out[i, 0], out[i, 1] = combine(p, n, k, live)


def level0(color, base, count, src, gidx, rank, bufs, w):
    _, _, n, rows = bufs[0].shape
    k = w.shape[-2]
    return call(
        functools.partial(level0_body, color, base, count),
        [src, gidx, rank], [*bufs, w],
        jax.ShapeDtypeStruct((count, 2, n, k), BF16),
        8 * count * n * k * rows, 4 << 20,
        [
            pltpu.VMEM((count, 2, n, rows), BF16),
            pltpu.VMEM((count, 2, k, rows), BF16),
            pltpu.SemaphoreType.DMA((2, count)),
        ],
        space=[pltpu.HBM] * 17,
        room=count * 2 * rows * (n + k) * 2,
    )


def combine(p, n, k, live):
    zero = jnp.zeros((n, k), F32)
    real = jnp.where(live, p[:n, :k] - p[n:, k:], zero).astype(BF16)
    imag = jnp.where(live, p[n:, :k] + p[:n, k:], zero).astype(BF16)
    return real, imag


def section_copies(base, own, other, ws, levels, weights, sems):
    def copies(i):
        pairs = [(own.at[i], levels.at[0, i]), (other.at[i], levels.at[1, i])]
        pairs += [(w.at[0, 0, base + i], weights.at[j, i]) for j, w in enumerate(ws)]
        return [pltpu.make_async_copy(a, b, sems.at[j, i]) for j, (a, b) in enumerate(pairs)]

    return copies


def section_apply(i, f, upper, rank, levels, weights):
    _, _, _, n, k = levels.shape
    a = levels[0, i].reshape(2 * n, k)
    b = levels[1, i].reshape(2 * n, k)
    x = jnp.concatenate([jnp.where(upper, b, a), jnp.where(upper, a, b)], axis=1)
    live = lax.broadcasted_iota(jnp.int32, (n, k), 1) < rank[0, f]
    for j in range(weights.shape[0]):
        yield combine(nt(x, weights[j, i].reshape(2 * k, 2 * k)), n, k, live)


def section_scratch(count, n, k, parts):
    return [
        pltpu.VMEM((2, count, 2, n, k), BF16),
        pltpu.VMEM((parts, count, 2, k, 2 * k), BF16),
        pltpu.SemaphoreType.DMA((2 + parts, count)),
    ], 8 * count * n * k + 8 * parts * count * k * k


def section_body(base, parts, bit, rank, own, other, *refs):
    ws, outs, (levels, weights, sems) = refs[:parts], refs[parts : 2 * parts], refs[2 * parts :]
    count = own.shape[0]
    copies = section_copies(base, own, other, ws, levels, weights, sems)
    for i in range(count):
        for c in copies(i):
            c.start()
    for i in range(count):
        for c in copies(i):
            c.wait()
        got = section_apply(i, base + i, bit[0] == 1, rank, levels, weights)
        for out, (real, imag) in zip(outs, got):
            out[i, 0], out[i, 1] = real, imag


def section(base, bit, rank, own, other, ws):
    count, _, n, k = own.shape
    shape = jax.ShapeDtypeStruct(own.shape, BF16)
    scratch, room = section_scratch(count, n, k, len(ws))
    return call(
        functools.partial(section_body, base, len(ws)),
        [bit, rank], [own, other, *ws], [shape] * len(ws),
        16 * count * n * k * k * len(ws), 3 << 20,
        scratch, space=[pltpu.HBM] * (2 + len(ws)), room=room,
    )


def fill(xs, f, real, imag):
    n = real.shape[0]
    xs[f, :n] = jnp.concatenate([real, -imag], 1)
    xs[f, n:] = jnp.concatenate([imag, real], 1)


def outward_blocks(dtype, order, xs, w, out, ws, sems):
    n = xs.shape[1] // 2
    blocks, step = ws.shape[0], ws.shape[3]
    piece = out.shape[3]
    per = piece // step

    def copy(b):
        start = pl.multiple_of(order[b // per] * piece + (b % per) * step, step)
        return pltpu.make_async_copy(w.at[0, 0, :, :, pl.ds(start, step)], ws.at[b], sems.at[b])

    def begin():
        copy(0).start()
        copy(1).start()

    def body(b, carry):
        copy(b).wait()

        @pl.when(b + 2 < blocks)
        def _():
            copy(b + 2).start()

        acc = jnp.zeros((2 * n, step), F32)
        for f in range(xs.shape[0]):
            acc += nt(xs[f], jnp.concatenate([ws[b, f, 0], ws[b, f, 1]], 1))
        to = pl.ds(pl.multiple_of((b % per) * step, step), step)
        out[b // per, 0, :, to] = acc[:n].astype(dtype)
        out[b // per, 1, :, to] = acc[n:].astype(dtype)
        return carry

    return begin, lambda: lax.fori_loop(0, blocks, body, 0)


def outward_body(dtype, order, xs, w, out, ws, sems):
    begin, rest = outward_blocks(dtype, order, xs, w, out, ws, sems)
    begin()
    rest()


def outward_scratch(count, n, w, step=256):
    _, _, far, _, size_out, k = w.shape
    piece = size_out // 4
    blocks = count * piece // step
    return (
        (count, 2, n, piece),
        [pltpu.VMEM((blocks, far, 2, step, k), BF16), pltpu.SemaphoreType.DMA((blocks,))],
        blocks * far * step * k * 4,
        8 * far * n * k * piece * count,
    )


def outward(dtype, order, xs, w):
    shape, scratch, room, flops = outward_scratch(order.shape[0], xs.shape[1] // 2, w)
    return call(
        functools.partial(outward_body, dtype),
        [order], [xs, w], jax.ShapeDtypeStruct(shape, dtype), flops, 4 << 20,
        scratch, space=[pltpu.VMEM, pltpu.HBM], room=room,
    )


def level2_outward_body(base, order, bit, rank, ready, own, other, s2, w, xs, out, *scratch):
    levels, weights, sems, ws, wsems = scratch
    copies = section_copies(base, own, other, [s2], levels, weights, sems)
    count = own.shape[0]
    for i in range(count):
        for c in copies(i):
            c.start()
    begin, rest = outward_blocks(BF16, order, xs, w, out, ws, wsems)
    begin()
    for i in range(base):
        fill(xs, i, ready[i, 0], ready[i, 1])
    for i in range(count):
        for c in copies(i):
            c.wait()
        for real, imag in section_apply(i, base + i, bit[0] == 1, rank, levels, weights):
            fill(xs, base + i, real, imag)
    rest()


def level2_outward(order, bit, rank, ready, own, other, s2, w):
    count, _, n, k = own.shape
    base = ready.shape[0]
    far = base + count
    scratch, room = section_scratch(count, n, k, 1)
    shape, more, more_room, flops = outward_scratch(order.shape[0], n, w)
    return call(
        functools.partial(level2_outward_body, base),
        [order, bit, rank], [ready, own, other, s2, w],
        [jax.ShapeDtypeStruct((far, 2 * n, 2 * k), BF16), jax.ShapeDtypeStruct(shape, BF16)],
        flops, 6 << 20,
        scratch + more, space=[pltpu.VMEM] + [pltpu.HBM] * 4, room=room + more_room,
    )


def final_body(first, base, last, out):
    n = first.shape[1]
    out[:, :n] = first[...]
    out[:, n:] = (base[...] + last[...].astype(F32)).astype(BF16)


def final(first, base, last):
    parts, n, rows = first.shape
    return call(
        final_body, [], [first, base, last],
        jax.ShapeDtypeStruct((parts, 2 * n, rows), BF16), 1 << 18, 1 << 20,
    )


def gather(color, block):
    one, two = ("x", "y") if color == 0 else ("y", "x")
    below = ring(block, one, 1)
    above = ring(block, one, -1)
    opposite = ring(block, one, 2)
    lo = jnp.concatenate([block, below], 0)
    hi = jnp.concatenate([above, opposite], 0)
    below_lo = ring(lo, two, 1)
    above_hi = ring(hi, two, -1)
    below_hi = ring(hi, two, 1)
    above_lo = ring(lo, two, -1)
    far_lo = ring(below_lo, two, 1)
    far_hi = ring(above_hi, two, -1)
    mine = [lo, hi, below_lo, below_hi, above_lo, above_hi, far_lo, far_hi]
    return mine + [swap(v, "grp", 1) for v in mine]


def on_device(
    incident,
    near_blocks,
    near_mask,
    far_source,
    far_rank,
    basis_in,
    section_one,
    section_two,
    basis_out,
):
    _, nrhs, rows = incident.shape
    leaf = near_blocks.shape[3]
    far = basis_in.shape[2]
    q = nrhs // 4
    member = lax.axis_index("mem")
    gidx = lax.axis_index("grp").reshape(1).astype(jnp.int32)

    bufs = [gather(c, incident[None, :, 2 * c * q : 2 * (c + 1) * q]) for c in range(2)]
    section_pair = swap(section_one, "mem", 1)

    axes = ("grp", "mem")
    total = lax.axis_size("grp") * lax.axis_size("mem")
    forward = [(i, i + 1) for i in range(total - 1)]
    backward = [(i + 1, i) for i in range(total - 1)]
    low = lax.ppermute(incident[:, :, rows - leaf :], axes, forward)
    high = lax.ppermute(incident[:, :, :leaf], axes, backward)
    near = near_field(near_mask, incident, low, high, near_blocks)

    bit0 = (member & 1).reshape(1).astype(jnp.int32)
    bit1 = (member >> 1).reshape(1).astype(jnp.int32)
    far_near = jnp.array([2, 1, 3, 0], jnp.int32)
    cut = far // 2
    spans = ((0, cut), (cut, far - cut))

    pieces = []
    for h in range(2):
        at = slice(2 * h * q, 2 * (h + 1) * q)
        level1 = []
        for base, count in spans:
            lev0 = level0(h, base, count, far_source, gidx, far_rank, bufs[h], basis_in)
            lev0_pair = swap(lev0, "mem", 1)
            lev1, lev1_pair = section(
                base, bit0, far_rank, lev0, lev0_pair, [section_one, section_pair]
            )
            level1.append((lev1, swap(lev1_pair, "mem", 3)))
        (ready,) = section(0, bit1, far_rank, *level1[0], [section_two])
        early = 2 - h
        xs, sent = level2_outward(
            member ^ far_near[:early], bit1, far_rank, ready, *level1[1],
            section_two, basis_out,
        )
        sent = swap(sent, "mem", 1)
        if h == 0:
            sent = (sent[0], sent[1])
        else:
            part = outward(BF16, member ^ far_near[1:2], xs, basis_out)
            sent = (sent[0], swap(part, "mem", 1)[0])
        other = outward(F32, member ^ far_near[2:3], xs, basis_out)[0]
        last = swap((other + sent[0].astype(F32)).astype(BF16), "mem", 3)
        kept = outward(F32, member ^ far_near[3:], xs, basis_out)[0]
        pieces.append((kept + sent[1].astype(F32) + near[:, at], last))
    base, last = pieces[0]
    return final((base + last.astype(F32)).astype(BF16), *pieces[1])


def solution(mesh):
    placed = (
        P(None, None, ("grp", "mem")),
        P(("grp", "mem"), None, None, None, None),
        P(("grp", "mem"), None),
        P(),
        P("grp", None),
        P("grp", "mem", None, None, None, None),
        P("grp", "mem", None, None, None, None),
        P("grp", "mem", None, None, None, None),
        P("grp", "mem", None, None, None, None),
    )

    return jax.shard_map(
        on_device,
        mesh=mesh,
        in_specs=placed,
        out_specs=P(None, None, ("grp", "mem")),
        check_vma=False,
    )
```

```python
import functools

import jax
import jax.numpy as jnp
from jax import lax
from jax.experimental import pallas as pl
from jax.experimental.pallas import tpu as pltpu
from jax.sharding import PartitionSpec as P


F32 = jnp.float32
BF16 = jnp.bfloat16
SIDE = 4
SHIFT = {"x": 1, "y": 3}


def swap(value, axis, mask):
    return lax.ppermute(value, axis, [(i, i ^ mask) for i in range(lax.axis_size(axis))])


def ring(value, axis, by):
    at = SHIFT[axis]
    perm = []
    for i in range(lax.axis_size("grp")):
        v = (i >> at) & (SIDE - 1)
        perm.append((i, i + ((((v + by) % SIDE) - v) << at)))
    return lax.ppermute(value, "grp", perm)


def nt(left, right):
    return lax.dot_general(left, right, (((1,), (1,)), ((), ())), preferred_element_type=F32)


VMEM = pl.BlockSpec(memory_space=pltpu.VMEM)
SMEM = pl.BlockSpec(memory_space=pltpu.SMEM)


def size(v):
    return v.size * v.dtype.itemsize


def call(body, scalars, arrays, out_shape, scratch=(), space=None, room=0):
    space = space or [pltpu.VMEM] * len(arrays)
    inside = [v for v, at in zip(arrays, space) if at == pltpu.VMEM]
    room += sum(size(v) for v in jax.tree.leaves(out_shape) + inside) + (2 << 20)
    return pl.pallas_call(
        body,
        in_specs=[SMEM] * len(scalars) + [pl.BlockSpec(memory_space=at) for at in space],
        out_specs=jax.tree.map(lambda _: VMEM, out_shape),
        out_shape=out_shape,
        scratch_shapes=scratch,
        compiler_params=pltpu.CompilerParams(vmem_limit_bytes=room),
        cost_estimate=pl.CostEstimate(flops=0, bytes_accessed=0, transcendentals=0),
    )(
        *scalars,
        *(
            pltpu.with_memory_space_constraint(v, at) if at == pltpu.HBM else v
            for v, at in zip(arrays, space)
        ),
    )


def near_body(mask, x, low, high, blocks, out):
    nrhs = x.shape[1]
    leaf = blocks.shape[-1]
    rows = nrhs // 4

    def step(t, carry):
        at = pl.ds(pl.multiple_of(t * rows, rows), rows)
        seq = [low[:, at, :]]
        seq += [x[:, at, i * leaf : (i + 1) * leaf] for i in range(2)]
        seq += [high[:, at, :]]
        seq = [v.reshape(2 * rows, leaf) for v in seq]
        for i in range(2):
            real = jnp.zeros((rows, leaf), F32)
            imag = jnp.zeros((rows, leaf), F32)
            for j in range(3):
                p = nt(seq[i + j], blocks[i, j].reshape(2 * leaf, leaf))
                w = mask[i, j].astype(F32)
                real += w * (p[:rows, :leaf] - p[rows:, leaf:])
                imag += w * (p[rows:, :leaf] + p[:rows, leaf:])
            out[0, at, i * leaf : (i + 1) * leaf] = real
            out[1, at, i * leaf : (i + 1) * leaf] = imag
        return carry

    lax.fori_loop(0, 4, step, 0)


def near_field(mask, x, low, high, blocks):
    _, nrhs, rows = x.shape
    return call(
        near_body, [mask], [x, low, high, blocks],
        jax.ShapeDtypeStruct((2, nrhs, rows), F32),
    )


def level0_body(color, base, count, src, rank, *refs):
    bufs, w, out = refs[:16], refs[16], refs[17]
    xs, sems = refs[18:]
    me = lax.axis_index("grp")
    k = w.shape[-2]
    n = xs.shape[2]

    def fetch(i, carry):
        f = i + base
        s = src[f, me]
        dx = (((s >> 1) & 3) - ((me >> 1) & 3)) & 3
        dy = (((s >> 3) & 3) - ((me >> 3) & 3)) & 3
        dx, dy = (jnp.where(v == 0, 0, jnp.where(v == 3, 1, v + 1)) for v in (dx, dy))
        first, second = (dx, dy) if color == 0 else (dy, dx)
        which = 2 * second + (first >> 1) + 8 * ((s ^ me) & 1)
        for t in range(16):

            @pl.when(which == t)
            def _():
                pltpu.make_async_copy(bufs[t].at[first & 1], xs.at[i], sems.at[i]).start()

        return carry

    lax.fori_loop(0, count, fetch, 0)
    for i in range(count):
        pltpu.make_async_copy(bufs[0].at[0], xs.at[i], sems.at[i]).wait()
        p = nt(xs[i].reshape(2 * n, xs.shape[3]), w[0, 0, base + i].reshape(2 * k, w.shape[-1]))
        live = lax.broadcasted_iota(jnp.int32, (n, k), 1) < rank[0, base + i]
        out[i, 0], out[i, 1] = combine(p, n, k, live)


def level0(color, base, count, src, rank, bufs, w):
    _, _, n, rows = bufs[0].shape
    k = w.shape[-2]
    return call(
        functools.partial(level0_body, color, base, count),
        [src, rank], [*bufs, w],
        jax.ShapeDtypeStruct((count, 2, n, k), BF16),
        [
            pltpu.VMEM((count, 2, n, rows), BF16),
            pltpu.SemaphoreType.DMA((count,)),
        ],
        space=[pl.ANY] * 16 + [pltpu.VMEM],
        room=count * 2 * rows * n * 2,
    )


def combine(p, n, k, live):
    zero = jnp.zeros((n, k), F32)
    real = jnp.where(live, p[:n, :k] - p[n:, k:], zero).astype(BF16)
    imag = jnp.where(live, p[n:, :k] + p[:n, k:], zero).astype(BF16)
    return real, imag


def section_body(base, bit, rank, own, other, *refs):
    upper = (lax.axis_index("mem") >> bit) & 1 == 1
    half = len(refs) // 2
    ws, outs = refs[:half], refs[half:]
    count, _, n, k = own.shape
    for i in range(count):
        a = own[i].reshape(2 * n, k)
        b = other[i].reshape(2 * n, k)
        x = jnp.concatenate([jnp.where(upper, b, a), jnp.where(upper, a, b)], axis=1)
        live = lax.broadcasted_iota(jnp.int32, (n, k), 1) < rank[0, base + i]
        for w, out in zip(ws, outs):
            p = nt(x, w[0, 0, base + i].reshape(2 * k, 2 * k))
            out[i, 0], out[i, 1] = combine(p, n, k, live)


def section(base, bit, rank, own, other, ws):
    shape = jax.ShapeDtypeStruct(own.shape, BF16)
    return call(
        functools.partial(section_body, base, bit),
        [rank], [own, other, *ws], [shape] * len(ws),
    )


def fill(xs, f, real, imag):
    n = real.shape[0]
    xs[f, :n] = jnp.concatenate([real, -imag], 1)
    xs[f, n:] = jnp.concatenate([imag, real], 1)


def outward_apply(dtype, order, xs, w, out):
    member = lax.axis_index("mem")
    n = xs.shape[1] // 2
    step = 256
    piece = out.shape[3]
    per = piece // step

    def body(b, carry):
        mask = order[0]
        for p in range(1, len(order)):
            mask = jnp.where(b // per == p, order[p], mask)
        start = pl.multiple_of((member ^ mask) * piece + (b % per) * step, step)
        rows = pl.ds(start, step)
        acc = jnp.zeros((2 * n, step), F32)
        for f in range(xs.shape[0]):
            acc += nt(xs[f], jnp.concatenate([w[0, 0, f, 0, rows], w[0, 0, f, 1, rows]], 1))
        to = pl.ds(pl.multiple_of((b % per) * step, step), step)
        out[b // per, 0, :, to] = acc[:n].astype(dtype)
        out[b // per, 1, :, to] = acc[n:].astype(dtype)
        return carry

    lax.fori_loop(0, out.shape[0] * per, body, 0)


def first_body(base, order, rank, ready, own, other, s2, w, xs, out):
    for i in range(base):
        fill(xs, i, ready[i, 0], ready[i, 1])
    count, _, n, k = own.shape
    upper = (lax.axis_index("mem") >> 1) & 1 == 1
    for i in range(count):
        a = own[i].reshape(2 * n, k)
        b = other[i].reshape(2 * n, k)
        x = jnp.concatenate([jnp.where(upper, b, a), jnp.where(upper, a, b)], axis=1)
        live = lax.broadcasted_iota(jnp.int32, (n, k), 1) < rank[0, base + i]
        p = nt(x, s2[0, 0, base + i].reshape(2 * k, 2 * k))
        fill(xs, base + i, *combine(p, n, k, live))
    outward_apply(BF16, order, xs, w, out)


def first_outward(order, rank, ready, own, other, s2, w):
    count, _, n, k = own.shape
    base = ready.shape[0]
    far = base + count
    return call(
        functools.partial(first_body, base, order),
        [rank], [ready, own, other, s2, w],
        [
            jax.ShapeDtypeStruct((far, 2 * n, 2 * k), BF16),
            jax.ShapeDtypeStruct((len(order), 2, n, w.shape[4] // 4), BF16),
        ],
    )


def outward(dtype, order, xs, w):
    shape = (len(order), 2, xs.shape[1] // 2, w.shape[4] // 4)
    return call(
        functools.partial(outward_apply, dtype, order),
        [], [xs, w], jax.ShapeDtypeStruct(shape, dtype),
    )


def final_body(first, base, last, out):
    n = first.shape[1]
    out[:, :n] = first[...]
    out[:, n:] = (base[...] + last[...].astype(F32)).astype(BF16)


def final(first, base, last):
    parts, n, rows = first.shape
    return call(
        final_body, [], [first, base, last],
        jax.ShapeDtypeStruct((parts, 2 * n, rows), BF16),
    )


def gather(color, block):
    one, two = ("x", "y") if color == 0 else ("y", "x")
    below = ring(block, one, 1)
    above = ring(block, one, -1)
    opposite = ring(block, one, 2)
    lo = jnp.concatenate([block, below], 0)
    hi = jnp.concatenate([above, opposite], 0)
    below_lo = ring(lo, two, 1)
    above_hi = ring(hi, two, -1)
    below_hi = ring(hi, two, 1)
    above_lo = ring(lo, two, -1)
    far_lo = ring(below_lo, two, 1)
    far_hi = ring(above_hi, two, -1)
    mine = [lo, hi, below_lo, below_hi, above_lo, above_hi, far_lo, far_hi]
    return mine + [swap(v, "grp", 1) for v in mine]


def on_device(
    incident,
    near_blocks,
    near_mask,
    far_source,
    far_rank,
    basis_in,
    section_one,
    section_two,
    basis_out,
):
    _, nrhs, rows = incident.shape
    leaf = near_blocks.shape[3]
    far = basis_in.shape[2]
    q = nrhs // 4

    bufs = [gather(c, incident[None, :, 2 * c * q : 2 * (c + 1) * q]) for c in range(2)]
    section_pair = swap(section_one, "mem", 1)

    axes = ("grp", "mem")
    total = lax.axis_size("grp") * lax.axis_size("mem")
    forward = [(i, i + 1) for i in range(total - 1)]
    backward = [(i + 1, i) for i in range(total - 1)]
    low = lax.ppermute(incident[:, :, rows - leaf :], axes, forward)
    high = lax.ppermute(incident[:, :, :leaf], axes, backward)
    near = near_field(near_mask, incident, low, high, near_blocks)

    cut = far // 2
    spans = ((0, cut), (cut, far - cut))

    pieces = []
    for h in range(2):
        at = slice(2 * h * q, 2 * (h + 1) * q)
        level1 = []
        for base, count in spans:
            lev0 = level0(h, base, count, far_source.T, far_rank, bufs[h], basis_in)
            lev0_pair = swap(lev0, "mem", 1)
            lev1, lev1_pair = section(
                base, 0, far_rank, lev0, lev0_pair, [section_one, section_pair]
            )
            level1.append((lev1, swap(lev1_pair, "mem", 3)))
        (ready,) = section(0, 1, far_rank, *level1[0], [section_two])
        early = 2 - h
        xs, sent = first_outward(
            (2, 1)[:early], far_rank, ready, *level1[1],
            section_two, basis_out,
        )
        sent = swap(sent, "mem", 1)
        if h == 0:
            sent = (sent[0], sent[1])
        else:
            part = outward(BF16, (1,), xs, basis_out)
            sent = (sent[0], swap(part, "mem", 1)[0])
        other = outward(F32, (3,), xs, basis_out)[0]
        last = swap((other + sent[0].astype(F32)).astype(BF16), "mem", 3)
        kept = outward(F32, (0,), xs, basis_out)[0]
        pieces.append((kept + sent[1].astype(F32) + near[:, at], last))
    base, last = pieces[0]
    return final((base + last.astype(F32)).astype(BF16), *pieces[1])


def solution(mesh):
    placed = (
        P(None, None, ("grp", "mem")),
        P(("grp", "mem"), None, None, None, None),
        P(("grp", "mem"), None),
        P(),
        P("grp", None),
        P("grp", "mem", None, None, None, None),
        P("grp", "mem", None, None, None, None),
        P("grp", "mem", None, None, None, None),
        P("grp", "mem", None, None, None, None),
    )

    return jax.shard_map(
        on_device,
        mesh=mesh,
        in_specs=placed,
        out_specs=P(None, None, ("grp", "mem")),
        check_vma=False,
    )
```

```python
import functools

import jax
import jax.numpy as jnp
from jax import lax
from jax.experimental import pallas as pl
from jax.experimental.pallas import tpu as pltpu
from jax.sharding import PartitionSpec as P


F32 = jnp.float32
BF16 = jnp.bfloat16
SIDE = 4
SHIFT = {"x": 1, "y": 3}


def swap(value, axis, mask):
    return lax.ppermute(value, axis, [(i, i ^ mask) for i in range(lax.axis_size(axis))])


def ring(value, axis, by):
    at = SHIFT[axis]
    perm = []
    for i in range(lax.axis_size("grp")):
        v = (i >> at) & (SIDE - 1)
        perm.append((i, i + ((((v + by) % SIDE) - v) << at)))
    return lax.ppermute(value, "grp", perm)


def nt(left, right):
    return lax.dot_general(left, right, (((1,), (1,)), ((), ())), preferred_element_type=F32)


VMEM = pl.BlockSpec(memory_space=pltpu.VMEM)
SMEM = pl.BlockSpec(memory_space=pltpu.SMEM)


def size(v):
    return v.size * v.dtype.itemsize


def call(body, scalars, arrays, out_shape, scratch=(), space=None, room=0):
    space = space or [pltpu.VMEM] * len(arrays)
    inside = [v for v, at in zip(arrays, space) if at == pltpu.VMEM]
    room += sum(size(v) for v in jax.tree.leaves(out_shape) + inside) + (2 << 20)
    return pl.pallas_call(
        body,
        in_specs=[SMEM] * len(scalars) + [pl.BlockSpec(memory_space=at) for at in space],
        out_specs=jax.tree.map(lambda _: VMEM, out_shape),
        out_shape=out_shape,
        scratch_shapes=scratch,
        compiler_params=pltpu.CompilerParams(vmem_limit_bytes=room),
        cost_estimate=pl.CostEstimate(flops=0, bytes_accessed=0, transcendentals=0),
    )(
        *scalars,
        *(
            pltpu.with_memory_space_constraint(v, at) if at == pltpu.HBM else v
            for v, at in zip(arrays, space)
        ),
    )


def near_body(mask, x, low, high, blocks, out):
    nrhs = x.shape[1]
    leaf = blocks.shape[-1]
    rows = nrhs // 4

    def step(t, carry):
        at = pl.ds(pl.multiple_of(t * rows, rows), rows)
        seq = [low[:, at, :]]
        seq += [x[:, at, i * leaf : (i + 1) * leaf] for i in range(2)]
        seq += [high[:, at, :]]
        seq = [v.reshape(2 * rows, leaf) for v in seq]
        for i in range(2):
            real = jnp.zeros((rows, leaf), F32)
            imag = jnp.zeros((rows, leaf), F32)
            for j in range(3):
                p = nt(seq[i + j], blocks[i, j].reshape(2 * leaf, leaf))
                w = mask[i, j].astype(F32)
                real += w * (p[:rows, :leaf] - p[rows:, leaf:])
                imag += w * (p[rows:, :leaf] + p[:rows, leaf:])
            out[0, at, i * leaf : (i + 1) * leaf] = real
            out[1, at, i * leaf : (i + 1) * leaf] = imag
        return carry

    lax.fori_loop(0, 4, step, 0)


def near_field(mask, x, low, high, blocks):
    _, nrhs, rows = x.shape
    return call(
        near_body, [mask], [x, low, high, blocks],
        jax.ShapeDtypeStruct((2, nrhs, rows), F32),
    )


def level0_body(color, base, count, src, rank, *refs):
    bufs, w, out = refs[:16], refs[16], refs[17]
    xs = refs[18]
    me = lax.axis_index("grp")
    k = w.shape[-2]
    n = xs.shape[2]

    def fetch(i, carry):
        f = i + base
        s = src[f, me]
        dx = (((s >> 1) & 3) - ((me >> 1) & 3)) & 3
        dy = (((s >> 3) & 3) - ((me >> 3) & 3)) & 3
        dx, dy = (jnp.where(v == 0, 0, jnp.where(v == 3, 1, v + 1)) for v in (dx, dy))
        first, second = (dx, dy) if color == 0 else (dy, dx)
        which = 2 * second + (first >> 1) + 8 * ((s ^ me) & 1)
        for t in range(16):

            @pl.when(which == t)
            def _():
                xs[i] = bufs[t][first & 1]

        return carry

    lax.fori_loop(0, count, fetch, 0)
    for i in range(count):
        p = nt(xs[i].reshape(2 * n, xs.shape[3]), w[0, 0, base + i].reshape(2 * k, w.shape[-1]))
        live = lax.broadcasted_iota(jnp.int32, (n, k), 1) < rank[0, base + i]
        out[i, 0], out[i, 1] = combine(p, n, k, live)


def level0(color, base, count, src, rank, bufs, w):
    _, _, n, rows = bufs[0].shape
    k = w.shape[-2]
    return call(
        functools.partial(level0_body, color, base, count),
        [src, rank], [*bufs, w],
        jax.ShapeDtypeStruct((count, 2, n, k), BF16),
        [pltpu.VMEM((count, 2, n, rows), BF16)],
        room=count * 2 * rows * n * 2,
    )


def combine(p, n, k, live):
    zero = jnp.zeros((n, k), F32)
    real = jnp.where(live, p[:n, :k] - p[n:, k:], zero).astype(BF16)
    imag = jnp.where(live, p[n:, :k] + p[:n, k:], zero).astype(BF16)
    return real, imag


def section_body(base, bit, rank, own, other, *refs):
    upper = (lax.axis_index("mem") >> bit) & 1 == 1
    half = len(refs) // 2
    ws, outs = refs[:half], refs[half:]
    count, _, n, k = own.shape
    for i in range(count):
        a = own[i].reshape(2 * n, k)
        b = other[i].reshape(2 * n, k)
        x = jnp.concatenate([jnp.where(upper, b, a), jnp.where(upper, a, b)], axis=1)
        live = lax.broadcasted_iota(jnp.int32, (n, k), 1) < rank[0, base + i]
        for w, out in zip(ws, outs):
            p = nt(x, w[0, 0, base + i].reshape(2 * k, 2 * k))
            out[i, 0], out[i, 1] = combine(p, n, k, live)


def section(base, bit, rank, own, other, ws):
    shape = jax.ShapeDtypeStruct(own.shape, BF16)
    return call(
        functools.partial(section_body, base, bit),
        [rank], [own, other, *ws], [shape] * len(ws),
    )


def fill(xs, f, real, imag):
    n = real.shape[0]
    xs[f, :n] = jnp.concatenate([real, -imag], 1)
    xs[f, n:] = jnp.concatenate([imag, real], 1)


def outward_apply(dtype, order, xs, w, out):
    member = lax.axis_index("mem")
    n = xs.shape[1] // 2
    step = 256
    piece = out.shape[3]
    per = piece // step

    def body(b, carry):
        mask = order[0]
        for p in range(1, len(order)):
            mask = jnp.where(b // per == p, order[p], mask)
        start = pl.multiple_of((member ^ mask) * piece + (b % per) * step, step)
        rows = pl.ds(start, step)
        acc = jnp.zeros((2 * n, step), F32)
        for f in range(xs.shape[0]):
            acc += nt(xs[f], jnp.concatenate([w[0, 0, f, 0, rows], w[0, 0, f, 1, rows]], 1))
        to = pl.ds(pl.multiple_of((b % per) * step, step), step)
        out[b // per, 0, :, to] = acc[:n].astype(dtype)
        out[b // per, 1, :, to] = acc[n:].astype(dtype)
        return carry

    lax.fori_loop(0, out.shape[0] * per, body, 0)


def first_body(base, order, rank, ready, own, other, s2, w, xs, out):
    for i in range(base):
        fill(xs, i, ready[i, 0], ready[i, 1])
    count, _, n, k = own.shape
    upper = (lax.axis_index("mem") >> 1) & 1 == 1
    for i in range(count):
        a = own[i].reshape(2 * n, k)
        b = other[i].reshape(2 * n, k)
        x = jnp.concatenate([jnp.where(upper, b, a), jnp.where(upper, a, b)], axis=1)
        live = lax.broadcasted_iota(jnp.int32, (n, k), 1) < rank[0, base + i]
        p = nt(x, s2[0, 0, base + i].reshape(2 * k, 2 * k))
        fill(xs, base + i, *combine(p, n, k, live))
    outward_apply(BF16, order, xs, w, out)


def first_outward(order, rank, ready, own, other, s2, w):
    count, _, n, k = own.shape
    base = ready.shape[0]
    far = base + count
    return call(
        functools.partial(first_body, base, order),
        [rank], [ready, own, other, s2, w],
        [
            jax.ShapeDtypeStruct((far, 2 * n, 2 * k), BF16),
            jax.ShapeDtypeStruct((len(order), 2, n, w.shape[4] // 4), BF16),
        ],
    )


def outward(dtype, order, xs, w):
    shape = (len(order), 2, xs.shape[1] // 2, w.shape[4] // 4)
    return call(
        functools.partial(outward_apply, dtype, order),
        [], [xs, w], jax.ShapeDtypeStruct(shape, dtype),
    )


def final_body(first, base, last, out):
    n = first.shape[1]
    out[:, :n] = first[...]
    out[:, n:] = (base[...] + last[...].astype(F32)).astype(BF16)


def final(first, base, last):
    parts, n, rows = first.shape
    return call(
        final_body, [], [first, base, last],
        jax.ShapeDtypeStruct((parts, 2 * n, rows), BF16),
    )


def gather(color, block):
    one, two = ("x", "y") if color == 0 else ("y", "x")
    below = ring(block, one, 1)
    above = ring(block, one, -1)
    opposite = ring(block, one, 2)
    lo = jnp.concatenate([block, below], 0)
    hi = jnp.concatenate([above, opposite], 0)
    below_lo = ring(lo, two, 1)
    above_hi = ring(hi, two, -1)
    below_hi = ring(hi, two, 1)
    above_lo = ring(lo, two, -1)
    far_lo = ring(below_lo, two, 1)
    far_hi = ring(above_hi, two, -1)
    mine = [lo, hi, below_lo, below_hi, above_lo, above_hi, far_lo, far_hi]
    return mine + [swap(v, "grp", 1) for v in mine]


def on_device(
    incident,
    near_blocks,
    near_mask,
    far_source,
    far_rank,
    basis_in,
    section_one,
    section_two,
    basis_out,
):
    _, nrhs, rows = incident.shape
    leaf = near_blocks.shape[3]
    far = basis_in.shape[2]
    q = nrhs // 4

    bufs = [gather(c, incident[None, :, 2 * c * q : 2 * (c + 1) * q]) for c in range(2)]
    section_pair = swap(section_one, "mem", 1)

    axes = ("grp", "mem")
    total = lax.axis_size("grp") * lax.axis_size("mem")
    forward = [(i, i + 1) for i in range(total - 1)]
    backward = [(i + 1, i) for i in range(total - 1)]
    low = lax.ppermute(incident[:, :, rows - leaf :], axes, forward)
    high = lax.ppermute(incident[:, :, :leaf], axes, backward)
    near = near_field(near_mask, incident, low, high, near_blocks)

    cut = far // 2
    spans = ((0, cut), (cut, far - cut))

    pieces = []
    for h in range(2):
        at = slice(2 * h * q, 2 * (h + 1) * q)
        level1 = []
        for base, count in spans:
            lev0 = level0(h, base, count, far_source.T, far_rank, bufs[h], basis_in)
            lev0_pair = swap(lev0, "mem", 1)
            lev1, lev1_pair = section(
                base, 0, far_rank, lev0, lev0_pair, [section_one, section_pair]
            )
            level1.append((lev1, swap(lev1_pair, "mem", 3)))
        (ready,) = section(0, 1, far_rank, *level1[0], [section_two])
        early = 2 - h
        xs, sent = first_outward(
            (2, 1)[:early], far_rank, ready, *level1[1],
            section_two, basis_out,
        )
        sent = swap(sent, "mem", 1)
        if h == 0:
            sent = (sent[0], sent[1])
        else:
            part = outward(BF16, (1,), xs, basis_out)
            sent = (sent[0], swap(part, "mem", 1)[0])
        other = outward(F32, (3,), xs, basis_out)[0]
        last = swap((other + sent[0].astype(F32)).astype(BF16), "mem", 3)
        kept = outward(F32, (0,), xs, basis_out)[0]
        pieces.append((kept + sent[1].astype(F32) + near[:, at], last))
    base, last = pieces[0]
    return final((base + last.astype(F32)).astype(BF16), *pieces[1])


def solution(mesh):
    placed = (
        P(None, None, ("grp", "mem")),
        P(("grp", "mem"), None, None, None, None),
        P(("grp", "mem"), None),
        P(),
        P("grp", None),
        P("grp", "mem", None, None, None, None),
        P("grp", "mem", None, None, None, None),
        P("grp", "mem", None, None, None, None),
        P("grp", "mem", None, None, None, None),
    )

    return jax.shard_map(
        on_device,
        mesh=mesh,
        in_specs=placed,
        out_specs=P(None, None, ("grp", "mem")),
        check_vma=False,
    )
```

```python
import functools

import jax
import jax.numpy as jnp
from jax import lax
from jax.experimental import pallas as pl
from jax.experimental.pallas import tpu as pltpu
from jax.sharding import PartitionSpec as P


F32 = jnp.float32
BF16 = jnp.bfloat16
SIDE = 4
SHIFT = {"x": 1, "y": 3}


def swap(value, axis, mask):
    return lax.ppermute(value, axis, [(i, i ^ mask) for i in range(lax.axis_size(axis))])


def ring(value, axis, by):
    at = SHIFT[axis]
    perm = []
    for i in range(lax.axis_size("grp")):
        v = (i >> at) & (SIDE - 1)
        perm.append((i, i + ((((v + by) % SIDE) - v) << at)))
    return lax.ppermute(value, "grp", perm)


def nt(left, right):
    return lax.dot_general(left, right, (((1,), (1,)), ((), ())), preferred_element_type=F32)


VMEM = pl.BlockSpec(memory_space=pltpu.VMEM)
SMEM = pl.BlockSpec(memory_space=pltpu.SMEM)


def size(v):
    return v.size * v.dtype.itemsize


def call(body, scalars, arrays, out_shape, scratch=(), space=None, room=0):
    space = space or [pltpu.VMEM] * len(arrays)
    inside = [v for v, at in zip(arrays, space) if at == pltpu.VMEM]
    room += sum(size(v) for v in jax.tree.leaves(out_shape) + inside) + (2 << 20)
    return pl.pallas_call(
        body,
        in_specs=[SMEM] * len(scalars) + [pl.BlockSpec(memory_space=at) for at in space],
        out_specs=jax.tree.map(lambda _: VMEM, out_shape),
        out_shape=out_shape,
        scratch_shapes=scratch,
        compiler_params=pltpu.CompilerParams(vmem_limit_bytes=room),
        cost_estimate=pl.CostEstimate(flops=0, bytes_accessed=0, transcendentals=0),
    )(
        *scalars,
        *(
            pltpu.with_memory_space_constraint(v, at) if at == pltpu.HBM else v
            for v, at in zip(arrays, space)
        ),
    )


def near_body(mask, x, low, high, blocks, out):
    nrhs = x.shape[1]
    leaf = blocks.shape[-1]
    rows = nrhs // 4

    def step(t, carry):
        at = pl.ds(pl.multiple_of(t * rows, rows), rows)
        seq = [low[:, at, :]]
        seq += [x[:, at, i * leaf : (i + 1) * leaf] for i in range(2)]
        seq += [high[:, at, :]]
        seq = [v.reshape(2 * rows, leaf) for v in seq]
        for i in range(2):
            real = jnp.zeros((rows, leaf), F32)
            imag = jnp.zeros((rows, leaf), F32)
            for j in range(3):
                p = nt(seq[i + j], blocks[i, j].reshape(2 * leaf, leaf))
                w = mask[i, j].astype(F32)
                real += w * (p[:rows, :leaf] - p[rows:, leaf:])
                imag += w * (p[rows:, :leaf] + p[:rows, leaf:])
            out[0, at, i * leaf : (i + 1) * leaf] = real
            out[1, at, i * leaf : (i + 1) * leaf] = imag
        return carry

    lax.fori_loop(0, 4, step, 0)


def near_field(mask, x, low, high, blocks):
    _, nrhs, rows = x.shape
    return call(
        near_body, [mask], [x, low, high, blocks],
        jax.ShapeDtypeStruct((2, nrhs, rows), F32),
    )


def level0_body(color, base, count, part, src, rank, *refs):
    bufs, w, out = refs[:16], refs[16], refs[17]
    xs = refs[18]
    me = lax.axis_index("grp")
    k = w.shape[-2]
    n = xs.shape[2]

    def fetch(i, carry):
        f = i + base
        s = src[f, me]
        dx = (((s >> 1) & 3) - ((me >> 1) & 3)) & 3
        dy = (((s >> 3) & 3) - ((me >> 3) & 3)) & 3
        dx, dy = (jnp.where(v == 0, 0, jnp.where(v == 3, 1, v + 1)) for v in (dx, dy))
        first, second = (dx, dy) if color == 0 else (dy, dx)
        which = 2 * second + (first >> 1) + 8 * ((s ^ me) & 1)
        for t in range(16):

            @pl.when(which == t)
            def _():
                xs[i] = bufs[t][first & 1, :, part]

        return carry

    lax.fori_loop(0, count, fetch, 0)
    for i in range(count):
        p = nt(xs[i].reshape(2 * n, xs.shape[3]), w[0, 0, base + i].reshape(2 * k, w.shape[-1]))
        live = lax.broadcasted_iota(jnp.int32, (n, k), 1) < rank[0, base + i]
        out[i, 0], out[i, 1] = combine(p, n, k, live)


def level0(color, base, count, part, src, rank, bufs, w):
    rows = bufs[0].shape[3]
    n = part.stop - part.start
    k = w.shape[-2]
    return call(
        functools.partial(level0_body, color, base, count, part),
        [src, rank], [*bufs, w],
        jax.ShapeDtypeStruct((count, 2, n, k), BF16),
        [pltpu.VMEM((count, 2, n, rows), BF16)],
        room=count * 2 * rows * n * 2,
    )


def combine(p, n, k, live):
    zero = jnp.zeros((n, k), F32)
    real = jnp.where(live, p[:n, :k] - p[n:, k:], zero).astype(BF16)
    imag = jnp.where(live, p[n:, :k] + p[:n, k:], zero).astype(BF16)
    return real, imag


def section_body(base, bit, rank, own, other, *refs):
    upper = (lax.axis_index("mem") >> bit) & 1 == 1
    half = len(refs) // 2
    ws, outs = refs[:half], refs[half:]
    count, _, n, k = own.shape
    for i in range(count):
        a = own[i].reshape(2 * n, k)
        b = other[i].reshape(2 * n, k)
        x = jnp.concatenate([jnp.where(upper, b, a), jnp.where(upper, a, b)], axis=1)
        live = lax.broadcasted_iota(jnp.int32, (n, k), 1) < rank[0, base + i]
        for w, out in zip(ws, outs):
            p = nt(x, w[0, 0, base + i].reshape(2 * k, 2 * k))
            out[i, 0], out[i, 1] = combine(p, n, k, live)


def section(base, bit, rank, own, other, ws):
    shape = jax.ShapeDtypeStruct(own.shape, BF16)
    return call(
        functools.partial(section_body, base, bit),
        [rank], [own, other, *ws], [shape] * len(ws),
    )


def fill(xs, f, real, imag):
    n = real.shape[0]
    xs[f, :n] = jnp.concatenate([real, -imag], 1)
    xs[f, n:] = jnp.concatenate([imag, real], 1)


def outward_apply(dtype, order, xs, w, out):
    member = lax.axis_index("mem")
    n = xs.shape[1] // 2
    step = 256
    piece = out.shape[3]
    per = piece // step

    def body(b, carry):
        mask = order[0]
        for p in range(1, len(order)):
            mask = jnp.where(b // per == p, order[p], mask)
        start = pl.multiple_of((member ^ mask) * piece + (b % per) * step, step)
        rows = pl.ds(start, step)
        acc = jnp.zeros((2 * n, step), F32)
        for f in range(xs.shape[0]):
            acc += nt(xs[f], jnp.concatenate([w[0, 0, f, 0, rows], w[0, 0, f, 1, rows]], 1))
        to = pl.ds(pl.multiple_of((b % per) * step, step), step)
        out[b // per, 0, :, to] = acc[:n].astype(dtype)
        out[b // per, 1, :, to] = acc[n:].astype(dtype)
        return carry

    lax.fori_loop(0, out.shape[0] * per, body, 0)


def first_body(base, order, rank, *refs):
    ready, (own, other, s2, w, xs, out) = refs[:-6], refs[-6:]
    for i in range(base):
        fill(xs, i, ready[0][i, 0], ready[0][i, 1])
    count, _, n, k = own.shape
    upper = (lax.axis_index("mem") >> 1) & 1 == 1
    for i in range(count):
        a = own[i].reshape(2 * n, k)
        b = other[i].reshape(2 * n, k)
        x = jnp.concatenate([jnp.where(upper, b, a), jnp.where(upper, a, b)], axis=1)
        live = lax.broadcasted_iota(jnp.int32, (n, k), 1) < rank[0, base + i]
        p = nt(x, s2[0, 0, base + i].reshape(2 * k, 2 * k))
        fill(xs, base + i, *combine(p, n, k, live))
    outward_apply(BF16, order, xs, w, out)


def first_outward(order, rank, ready, own, other, s2, w):
    count, _, n, k = own.shape
    base = ready[0].shape[0] if ready else 0
    far = base + count
    return call(
        functools.partial(first_body, base, order),
        [rank], [*ready, own, other, s2, w],
        [
            jax.ShapeDtypeStruct((far, 2 * n, 2 * k), BF16),
            jax.ShapeDtypeStruct((len(order), 2, n, w.shape[4] // 4), BF16),
        ],
    )


def outward(dtype, order, xs, w):
    shape = (len(order), 2, xs.shape[1] // 2, w.shape[4] // 4)
    return call(
        functools.partial(outward_apply, dtype, order),
        [], [xs, w], jax.ShapeDtypeStruct(shape, dtype),
    )


def final_body(*refs):
    done, (base, last, out) = refs[:-3], refs[-3:]
    at = 0
    for v in done:
        out[:, at : at + v.shape[1]] = v[...]
        at += v.shape[1]
    out[:, at:] = (base[...] + last[...].astype(F32)).astype(BF16)


def final(done, base, last):
    parts, n, rows = base.shape
    n += sum(v.shape[1] for v in done)
    return call(
        final_body, [], [*done, base, last],
        jax.ShapeDtypeStruct((parts, n, rows), BF16),
    )


def gather(color, block):
    one, two = ("x", "y") if color == 0 else ("y", "x")
    below = ring(block, one, 1)
    above = ring(block, one, -1)
    opposite = ring(block, one, 2)
    lo = jnp.concatenate([block, below], 0)
    hi = jnp.concatenate([above, opposite], 0)
    below_lo = ring(lo, two, 1)
    above_hi = ring(hi, two, -1)
    below_hi = ring(hi, two, 1)
    above_lo = ring(lo, two, -1)
    far_lo = ring(below_lo, two, 1)
    far_hi = ring(above_hi, two, -1)
    mine = [lo, hi, below_lo, below_hi, above_lo, above_hi, far_lo, far_hi]
    return mine + [swap(v, "grp", 1) for v in mine]


def on_device(
    incident,
    near_blocks,
    near_mask,
    far_source,
    far_rank,
    basis_in,
    section_one,
    section_two,
    basis_out,
):
    _, nrhs, rows = incident.shape
    leaf = near_blocks.shape[3]
    far = basis_in.shape[2]
    q = nrhs // 4

    bufs = [gather(c, incident[None, :, 2 * c * q : 2 * (c + 1) * q]) for c in range(2)]
    section_pair = swap(section_one, "mem", 1)

    axes = ("grp", "mem")
    total = lax.axis_size("grp") * lax.axis_size("mem")
    forward = [(i, i + 1) for i in range(total - 1)]
    backward = [(i + 1, i) for i in range(total - 1)]
    low = lax.ppermute(incident[:, :, rows - leaf :], axes, forward)
    high = lax.ppermute(incident[:, :, :leaf], axes, backward)
    near = near_field(near_mask, incident, low, high, near_blocks)

    def pair_levels(color, base, count, part):
        lev0 = level0(color, base, count, part, far_source.T, far_rank, bufs[color], basis_in)
        lev0_pair = swap(lev0, "mem", 1)
        lev1, lev1_pair = section(base, 0, far_rank, lev0, lev0_pair, [section_one, section_pair])
        return lev1, swap(lev1_pair, "mem", 3)

    def outgoing(at, split, ready, level1):
        xs, sent = first_outward(
            (2,) if split else (2, 1), far_rank, ready, *level1,
            section_two, basis_out,
        )
        sent = swap(sent, "mem", 1)
        if split:
            part = outward(BF16, (1,), xs, basis_out)
            sent = (sent[0], swap(part, "mem", 1)[0])
        else:
            sent = (sent[0], sent[1])
        other = outward(F32, (3,), xs, basis_out)[0]
        last = swap((other + sent[0].astype(F32)).astype(BF16), "mem", 3)
        kept = outward(F32, (0,), xs, basis_out)[0]
        return kept + sent[1].astype(F32) + near[:, at], last

    cut = far * 3 // 7
    half, first, second = slice(0, 2 * q), slice(0, q), slice(q, 2 * q)
    done = []
    level1 = pair_levels(0, 0, cut, half)
    (ready,) = section(0, 1, far_rank, *level1, [section_two])
    done.append(outgoing(half, False, [ready], pair_levels(0, cut, far - cut, half)))
    done.append(outgoing(slice(2 * q, 3 * q), False, [], pair_levels(1, 0, far, first)))
    base, last = outgoing(slice(3 * q, 4 * q), True, [], pair_levels(1, 0, far, second))
    return final([(b + v.astype(F32)).astype(BF16) for b, v in done], base, last)


def solution(mesh):
    placed = (
        P(None, None, ("grp", "mem")),
        P(("grp", "mem"), None, None, None, None),
        P(("grp", "mem"), None),
        P(),
        P("grp", None),
        P("grp", "mem", None, None, None, None),
        P("grp", "mem", None, None, None, None),
        P("grp", "mem", None, None, None, None),
        P("grp", "mem", None, None, None, None),
    )

    return jax.shard_map(
        on_device,
        mesh=mesh,
        in_specs=placed,
        out_specs=P(None, None, ("grp", "mem")),
        check_vma=False,
    )
```

```python
import functools

import jax
import jax.numpy as jnp
from jax import lax
from jax.experimental import pallas as pl
from jax.experimental.pallas import tpu as pltpu
from jax.sharding import PartitionSpec as P


F32 = jnp.float32
BF16 = jnp.bfloat16
SIDE = 4
SHIFT = {"x": 1, "y": 3}


def swap(value, axis, mask):
    return lax.ppermute(value, axis, [(i, i ^ mask) for i in range(lax.axis_size(axis))])


def ring(value, axis, by):
    at = SHIFT[axis]
    perm = []
    for i in range(lax.axis_size("grp")):
        v = (i >> at) & (SIDE - 1)
        perm.append((i, i + ((((v + by) % SIDE) - v) << at)))
    return lax.ppermute(value, "grp", perm)


def nt(left, right):
    return lax.dot_general(left, right, (((1,), (1,)), ((), ())), preferred_element_type=F32)


VMEM = pl.BlockSpec(memory_space=pltpu.VMEM)
SMEM = pl.BlockSpec(memory_space=pltpu.SMEM)


def size(v):
    return v.size * v.dtype.itemsize


def call(body, scalars, arrays, out_shape, scratch=(), space=None, room=0):
    space = space or [pltpu.VMEM] * len(arrays)
    inside = [v for v, at in zip(arrays, space) if at == pltpu.VMEM]
    room += sum(size(v) for v in jax.tree.leaves(out_shape) + inside) + (2 << 20)
    return pl.pallas_call(
        body,
        in_specs=[SMEM] * len(scalars) + [pl.BlockSpec(memory_space=at) for at in space],
        out_specs=jax.tree.map(lambda _: VMEM, out_shape),
        out_shape=out_shape,
        scratch_shapes=scratch,
        compiler_params=pltpu.CompilerParams(vmem_limit_bytes=room),
        cost_estimate=pl.CostEstimate(flops=0, bytes_accessed=0, transcendentals=0),
    )(
        *scalars,
        *(
            pltpu.with_memory_space_constraint(v, at) if at == pltpu.HBM else v
            for v, at in zip(arrays, space)
        ),
    )


def near_body(mask, x, low, high, blocks, out):
    nrhs = x.shape[1]
    leaf = blocks.shape[-1]
    rows = nrhs // 4

    def step(t, carry):
        at = pl.ds(pl.multiple_of(t * rows, rows), rows)
        seq = [low[:, at, :]]
        seq += [x[:, at, i * leaf : (i + 1) * leaf] for i in range(2)]
        seq += [high[:, at, :]]
        seq = [v.reshape(2 * rows, leaf) for v in seq]
        for i in range(2):
            real = jnp.zeros((rows, leaf), F32)
            imag = jnp.zeros((rows, leaf), F32)
            for j in range(3):
                p = nt(seq[i + j], blocks[i, j].reshape(2 * leaf, leaf))
                w = mask[i, j].astype(F32)
                real += w * (p[:rows, :leaf] - p[rows:, leaf:])
                imag += w * (p[rows:, :leaf] + p[:rows, leaf:])
            out[0, at, i * leaf : (i + 1) * leaf] = real
            out[1, at, i * leaf : (i + 1) * leaf] = imag
        return carry

    lax.fori_loop(0, 4, step, 0)


def near_field(mask, x, low, high, blocks):
    _, nrhs, rows = x.shape
    return call(
        near_body, [mask], [x, low, high, blocks],
        jax.ShapeDtypeStruct((2, nrhs, rows), F32),
    )


def level0_body(color, base, count, part, src, rank, *refs):
    bufs, w, out = refs[:16], refs[16], refs[17]
    xs = refs[18]
    me = lax.axis_index("grp")
    k = w.shape[-2]
    n = xs.shape[2]

    def fetch(i, carry):
        f = i + base
        s = src[f, me]
        dx = (((s >> 1) & 3) - ((me >> 1) & 3)) & 3
        dy = (((s >> 3) & 3) - ((me >> 3) & 3)) & 3
        dx, dy = (jnp.where(v == 0, 0, jnp.where(v == 3, 1, v + 1)) for v in (dx, dy))
        first, second = (dx, dy) if color == 0 else (dy, dx)
        which = 2 * second + (first >> 1) + 8 * ((s ^ me) & 1)
        for t in range(16):

            @pl.when(which == t)
            def _():
                xs[i] = bufs[t][first & 1, :, part]

        return carry

    lax.fori_loop(0, count, fetch, 0)
    for i in range(count):
        p = nt(xs[i].reshape(2 * n, xs.shape[3]), w[0, 0, base + i].reshape(2 * k, w.shape[-1]))
        live = lax.broadcasted_iota(jnp.int32, (n, k), 1) < rank[0, base + i]
        out[i, 0], out[i, 1] = combine(p, n, k, live)


def level0(color, base, count, part, src, rank, bufs, w):
    rows = bufs[0].shape[3]
    n = part.stop - part.start
    k = w.shape[-2]
    return call(
        functools.partial(level0_body, color, base, count, part),
        [src, rank], [*bufs, w],
        jax.ShapeDtypeStruct((count, 2, n, k), BF16),
        [pltpu.VMEM((count, 2, n, rows), BF16)],
        room=count * 2 * rows * n * 2,
    )


def combine(p, n, k, live):
    zero = jnp.zeros((n, k), F32)
    real = jnp.where(live, p[:n, :k] - p[n:, k:], zero).astype(BF16)
    imag = jnp.where(live, p[n:, :k] + p[:n, k:], zero).astype(BF16)
    return real, imag


def section_body(base, bit, rank, own, other, *refs):
    upper = (lax.axis_index("mem") >> bit) & 1 == 1
    half = len(refs) // 2
    ws, outs = refs[:half], refs[half:]
    count, _, n, k = own.shape
    for i in range(count):
        a = own[i].reshape(2 * n, k)
        b = other[i].reshape(2 * n, k)
        x = jnp.concatenate([jnp.where(upper, b, a), jnp.where(upper, a, b)], axis=1)
        live = lax.broadcasted_iota(jnp.int32, (n, k), 1) < rank[0, base + i]
        for w, out in zip(ws, outs):
            p = nt(x, w[0, 0, base + i].reshape(2 * k, 2 * k))
            out[i, 0], out[i, 1] = combine(p, n, k, live)


def section(base, bit, rank, own, other, ws):
    shape = jax.ShapeDtypeStruct(own.shape, BF16)
    return call(
        functools.partial(section_body, base, bit),
        [rank], [own, other, *ws], [shape] * len(ws),
    )


def fill(xs, f, real, imag):
    n = real.shape[0]
    xs[f, :n] = jnp.concatenate([real, -imag], 1)
    xs[f, n:] = jnp.concatenate([imag, real], 1)


def outward_apply(dtype, order, xs, w, out):
    member = lax.axis_index("mem")
    n = xs.shape[1] // 2
    step = 256
    piece = out.shape[3]
    per = piece // step

    def body(b, carry):
        mask = order[0]
        for p in range(1, len(order)):
            mask = jnp.where(b // per == p, order[p], mask)
        start = pl.multiple_of((member ^ mask) * piece + (b % per) * step, step)
        rows = pl.ds(start, step)
        acc = jnp.zeros((2 * n, step), F32)
        for f in range(xs.shape[0]):
            acc += nt(xs[f], jnp.concatenate([w[0, 0, f, 0, rows], w[0, 0, f, 1, rows]], 1))
        to = pl.ds(pl.multiple_of((b % per) * step, step), step)
        out[b // per, 0, :, to] = acc[:n].astype(dtype)
        out[b // per, 1, :, to] = acc[n:].astype(dtype)
        return carry

    lax.fori_loop(0, out.shape[0] * per, body, 0)


def first_body(base, order, rank, *refs):
    ready, (own, other, s2, w, xs, out) = refs[:-6], refs[-6:]
    for i in range(base):
        fill(xs, i, ready[0][i, 0], ready[0][i, 1])
    count, _, n, k = own.shape
    upper = (lax.axis_index("mem") >> 1) & 1 == 1
    for i in range(count):
        a = own[i].reshape(2 * n, k)
        b = other[i].reshape(2 * n, k)
        x = jnp.concatenate([jnp.where(upper, b, a), jnp.where(upper, a, b)], axis=1)
        live = lax.broadcasted_iota(jnp.int32, (n, k), 1) < rank[0, base + i]
        p = nt(x, s2[0, 0, base + i].reshape(2 * k, 2 * k))
        fill(xs, base + i, *combine(p, n, k, live))
    outward_apply(BF16, order, xs, w, out)


def first_outward(order, rank, ready, own, other, s2, w):
    count, _, n, k = own.shape
    base = ready[0].shape[0] if ready else 0
    far = base + count
    return call(
        functools.partial(first_body, base, order),
        [rank], [*ready, own, other, s2, w],
        [
            jax.ShapeDtypeStruct((far, 2 * n, 2 * k), BF16),
            jax.ShapeDtypeStruct((len(order), 2, n, w.shape[4] // 4), BF16),
        ],
    )


def outward(dtype, order, xs, w):
    shape = (len(order), 2, xs.shape[1] // 2, w.shape[4] // 4)
    return call(
        functools.partial(outward_apply, dtype, order),
        [], [xs, w], jax.ShapeDtypeStruct(shape, dtype),
    )


def final_body(*refs):
    done, (base, last, out) = refs[:-3], refs[-3:]
    at = 0
    for v in done:
        out[:, at : at + v.shape[1]] = v[...]
        at += v.shape[1]
    out[:, at:] = (base[...] + last[...].astype(F32)).astype(BF16)


def final(done, base, last):
    parts, n, rows = base.shape
    n += sum(v.shape[1] for v in done)
    return call(
        final_body, [], [*done, base, last],
        jax.ShapeDtypeStruct((parts, n, rows), BF16),
    )


def gather(color, block):
    one, two = ("x", "y") if color == 0 else ("y", "x")
    below = ring(block, one, 1)
    above = ring(block, one, -1)
    opposite = ring(block, one, 2)
    lo = jnp.concatenate([block, below], 0)
    hi = jnp.concatenate([above, opposite], 0)
    below_lo = ring(lo, two, 1)
    above_hi = ring(hi, two, -1)
    below_hi = ring(hi, two, 1)
    above_lo = ring(lo, two, -1)
    far_lo = ring(below_lo, two, 1)
    far_hi = ring(above_hi, two, -1)
    mine = [lo, hi, below_lo, below_hi, above_lo, above_hi, far_lo, far_hi]
    return mine + [swap(v, "grp", 1) for v in mine]


def on_device(
    incident,
    near_blocks,
    near_mask,
    far_source,
    far_rank,
    basis_in,
    section_one,
    section_two,
    basis_out,
):
    _, nrhs, rows = incident.shape
    leaf = near_blocks.shape[3]
    far = basis_in.shape[2]
    q = nrhs // 4

    bufs = [gather(c, incident[None, :, 2 * c * q : 2 * (c + 1) * q]) for c in range(2)]
    section_pair = swap(section_one, "mem", 1)

    axes = ("grp", "mem")
    total = lax.axis_size("grp") * lax.axis_size("mem")
    forward = [(i, i + 1) for i in range(total - 1)]
    backward = [(i + 1, i) for i in range(total - 1)]
    low = lax.ppermute(incident[:, :, rows - leaf :], axes, forward)
    high = lax.ppermute(incident[:, :, :leaf], axes, backward)
    near = near_field(near_mask, incident, low, high, near_blocks)

    def pair_levels(color, base, count, part):
        lev0 = level0(color, base, count, part, far_source.T, far_rank, bufs[color], basis_in)
        lev0_pair = swap(lev0, "mem", 1)
        (lev1_pair,) = section(base, 0, far_rank, lev0, lev0_pair, [section_pair])
        (lev1,) = section(base, 0, far_rank, lev0, lev0_pair, [section_one])
        return lev1, swap(lev1_pair, "mem", 3)

    def outgoing(at, split, ready, level1):
        xs, sent = first_outward(
            (2,) if split else (2, 1), far_rank, ready, *level1,
            section_two, basis_out,
        )
        sent = swap(sent, "mem", 1)
        if split:
            part = outward(BF16, (1,), xs, basis_out)
            sent = (sent[0], swap(part, "mem", 1)[0])
        else:
            sent = (sent[0], sent[1])
        other = outward(F32, (3,), xs, basis_out)[0]
        last = swap((other + sent[0].astype(F32)).astype(BF16), "mem", 3)
        kept = outward(F32, (0,), xs, basis_out)[0]
        return kept + sent[1].astype(F32) + near[:, at], last

    cut = far // 2
    half, first, second = slice(0, 2 * q), slice(0, q), slice(q, 2 * q)
    done = []
    level1 = pair_levels(0, 0, cut, half)
    (ready,) = section(0, 1, far_rank, *level1, [section_two])
    done.append(outgoing(half, False, [ready], pair_levels(0, cut, far - cut, half)))
    done.append(outgoing(slice(2 * q, 3 * q), False, [], pair_levels(1, 0, far, first)))
    base, last = outgoing(slice(3 * q, 4 * q), True, [], pair_levels(1, 0, far, second))
    return final([(b + v.astype(F32)).astype(BF16) for b, v in done], base, last)


def solution(mesh):
    placed = (
        P(None, None, ("grp", "mem")),
        P(("grp", "mem"), None, None, None, None),
        P(("grp", "mem"), None),
        P(),
        P("grp", None),
        P("grp", "mem", None, None, None, None),
        P("grp", "mem", None, None, None, None),
        P("grp", "mem", None, None, None, None),
        P("grp", "mem", None, None, None, None),
    )

    return jax.shard_map(
        on_device,
        mesh=mesh,
        in_specs=placed,
        out_specs=P(None, None, ("grp", "mem")),
        check_vma=False,
    )
```
